32 devices in a mesh: groups: 1, frame: 32 (over z, y, x, core).
Axes of the slice: x: 2, y: 2, z: 4, core: 2. Of those that a mesh axis runs over, the one named last changes fastest.
Arguments:
- feature_map: bfloat16 [32, 64, 128, 128], P('frame', 'groups'), may hold values from -6 to 6
- pixel_row: int32 [32, 128], P('frame', 'groups'), may hold values from 6 to 56
- pixel_column: int32 [32, 128], P('frame', 'groups'), may hold values from 6 to 120
- query_frame: int32 [128], P('groups'), may hold values from 0 to 31
- visible: int32 [32, 128], P(None, 'groups'), may hold values 0 or 1
- window_start: int32 [1], P('groups'), may hold values from 0 to 4095
- match_weight: bfloat16 [98, 384], replicated, may hold values from -0.625 to 0.625
- layer_gains: float32 [2, 2, 384], replicated, may hold values from 0.5 to 1.5
- joint_weight: bfloat16 [2, 384, 1152], replicated
- output_weight: bfloat16 [2, 384, 384], replicated, may hold values from -0.3125 to 0.3125
- expand_weight: bfloat16 [2, 384, 1536], replicated, may hold values from -0.3125 to 0.3125
- reduce_weight: bfloat16 [2, 1536, 384], replicated, may hold values from -0.15625 to 0.15625
Outputs:
- handed: bfloat16 [32, 128, 384], P('frame', 'groups')
The draws below stay inside these ranges and needn't reach their ends.
All inputs are finite; a program needn't handle non-finite values.
Results may differ from the reference program's by a relative error of at most 0.015.
Values may be sent and summed in bfloat16 or wider, within the bound.
No kernel may reach another device: no remote copies, remote signals or barrier semaphores. Data moves between devices by JAX's collectives and lax.ppermute only.
A program may use at most 128 MiB of HBM per device.

```python
import math
import jax
import jax.numpy as jnp
from jax import lax

D = 384
HEADS = 8
MLP = 1536
C = 128
PATCH = 7
H_MAP = 64
W_MAP = 128
FRAMES = 32
POINTS = 128
MATCHES = 98


def draw_joint_weight(key, part):
    first_key = jax.random.fold_in(key, 0)
    return (jax.random.normal(first_key, (2, D, 3 * D), jnp.float32) / math.sqrt(D)).astype(jnp.bfloat16)


def with_ends(values, own_key, smallest, largest):
    extent = values.shape
    index_at = [jax.random.randint(jax.random.fold_in(own_key, axis), (), 0, extent[axis]) for axis in range(len(extent))]
    values = values.at[tuple(index_at)].set(smallest)
    longest = extent.index(max(extent))
    index_at[longest] = (index_at[longest] + 1) % extent[longest]
    return values.at[tuple(index_at)].set(largest)


def shard_levels(rng, shape, cuts, low, high):
    factor_of, own = 1.0, jax.random.fold_in(rng, 6)
    for axis_at, blocks in cuts:
        draws = jnp.exp(jax.random.uniform(jax.random.fold_in(own, axis_at), (blocks,), jnp.float32, low / len(cuts), high / len(cuts)))
        factor_of = factor_of * jnp.repeat(draws, shape[axis_at] // blocks).reshape([-1 if axis == axis_at else 1 for axis in range(len(shape))])
    return factor_of


def normal_values(stream_key, extent, scale, most, cuts=(), kind=jnp.bfloat16):
    drawn = jax.random.normal(stream_key, extent, jnp.float32) * scale
    if len(cuts) > 0:
        drawn = shard_levels(stream_key, extent, cuts, -0.22, 0.18) * drawn
    return jnp.clip(drawn, min=-most, max=most).astype(kind)


def setup_inputs(seed: int = 0, part: int = 0) -> dict:
    arg_keys = jax.random.split(jax.random.key(seed), 13)
    part_splits = jax.random.split(jax.random.fold_in(arg_keys[12], part), 13)
    return {
        "feature_map": normal_values(part_splits[0], (FRAMES, H_MAP, W_MAP, C), 1.0, 6.0, ((0, 32),)),
        "pixel_row": with_ends(jax.random.randint(part_splits[1], (FRAMES, POINTS), 6, H_MAP - 7), jax.random.fold_in(part_splits[1], 1), 6, (H_MAP - 7) - 1).astype(jnp.int32),
        "pixel_column": with_ends(jax.random.randint(part_splits[2], (FRAMES, POINTS), 6, W_MAP - 7), jax.random.fold_in(part_splits[2], 1), 6, (W_MAP - 7) - 1).astype(jnp.int32),
        "query_frame": with_ends(jax.random.randint(part_splits[3], (POINTS,), 0, FRAMES), jax.random.fold_in(part_splits[3], 1), 0, FRAMES - 1).astype(jnp.int32),
        "visible": with_ends((jax.random.randint(part_splits[4], (FRAMES, POINTS), 0, 4) < 3).astype(jnp.int32), jax.random.fold_in(part_splits[4], 1), 0, 1),
        "window_start": jax.random.randint(part_splits[5], (1,), 0, 4096).astype(jnp.int32),
        "match_weight": normal_values(arg_keys[6], (MATCHES, D), MATCHES ** -0.5, 0.625),
        "layer_gains": jnp.clip(1.0 + 0.1 * jax.random.normal(arg_keys[7], (2, 2, D), jnp.float32), 0.5, 1.5),
        "joint_weight": draw_joint_weight(jax.random.fold_in(arg_keys[12], 71), part),
        "output_weight": normal_values(arg_keys[9], (2, D, D), D ** -0.5, 0.3125),
        "expand_weight": normal_values(arg_keys[10], (2, D, MLP), D ** -0.5, 0.3125),
        "reduce_weight": normal_values(arg_keys[11], (2, MLP, D), MLP ** -0.5, 0.15625),
    }


EPSILON = 1e-05

def normalize(values, weights):
    average = lax.optimization_barrier(jnp.mean(values, axis=-1, keepdims=True))
    centred = values - average
    variance = lax.optimization_barrier(jnp.mean(centred * centred, axis=-1, keepdims=True))
    return centred * lax.rsqrt(variance + EPSILON) * weights

def coarsen(feature_map):
    frames, height, breadth, channels = feature_map.shape
    shaped = feature_map.astype(jnp.float32).reshape(frames, height // 2, 2, breadth // 2, 2, channels)
    return (lax.optimization_barrier(jnp.sum(shaped, axis=(2, 4))) * 0.25).astype(jnp.bfloat16)

def time_embedding(absolute, features):
    half_way = features // 2
    frequency = jnp.exp(-math.log(10000.0) * jnp.arange(half_way, dtype=jnp.float32) / half_way)
    angles = absolute.astype(jnp.float32)[:, None] * frequency[None, :]
    return jnp.concatenate([jnp.sin(angles), jnp.cos(angles)], axis=-1)

def transformer_block(tokens, allowed, gain_pair, joint_weight, output_weight, expand_weight, reduce_weight):
    groups, length, features = tokens.shape
    per_head = features // HEADS
    stream = tokens.astype(jnp.float32)
    hidden = normalize(stream, gain_pair[0]).astype(jnp.bfloat16)
    projected = jnp.einsum('gsd,de->gse', hidden.astype(jnp.float32), joint_weight.astype(jnp.float32)).astype(jnp.bfloat16)
    queries = projected[..., :features].reshape(groups, length, HEADS, per_head).astype(jnp.float32)
    keyset = projected[..., features:2 * features].reshape(groups, length, HEADS, per_head).astype(jnp.float32)
    values = projected[..., 2 * features:].reshape(groups, length, HEADS, per_head).astype(jnp.float32)
    scores = jnp.einsum('gqhe,gkhe->ghqk', queries, keyset) / math.sqrt(per_head)
    diagonal = jnp.arange(length)[:, None] == jnp.arange(length)[None, :]
    permitted = allowed[:, None, None, :] | diagonal[None, None]
    scores = jnp.where(permitted, scores, -1e+30)
    attn_weights = jax.nn.softmax(scores, axis=-1).astype(jnp.bfloat16)
    attended = jnp.einsum('ghqk,gkhe->gqhe', attn_weights.astype(jnp.float32), values).astype(jnp.bfloat16)
    attended = attended.reshape(groups, length, features)
    stream = stream + jnp.einsum('gsd,de->gse', attended.astype(jnp.float32), output_weight.astype(jnp.float32))
    hidden = normalize(stream, gain_pair[1]).astype(jnp.bfloat16)
    widened = jax.nn.gelu(jnp.einsum('gsd,de->gse', hidden.astype(jnp.float32), expand_weight.astype(jnp.float32)), approximate=True).astype(jnp.bfloat16)
    return (stream + jnp.einsum('gse,ed->gsd', widened.astype(jnp.float32), reduce_weight.astype(jnp.float32))).astype(jnp.bfloat16)

def reference(feature_map, pixel_row, pixel_column, query_frame, visible, window_start, match_weight, layer_gains, joint_weight, output_weight, expand_weight, reduce_weight):
    frames, height, breadth, channels = feature_map.shape
    points = query_frame.shape[0]
    features = match_weight.shape[1]
    pooled = coarsen(feature_map)
    point_ids = jnp.arange(points, dtype=jnp.int32)
    query_row = pixel_row[query_frame, point_ids]
    query_column = pixel_column[query_frame, point_ids]
    fine_feat = feature_map[query_frame, query_row, query_column].astype(jnp.float32)
    coarse_feat = pooled[query_frame, query_row // 2, query_column // 2].astype(jnp.float32)
    cells = jnp.arange(PATCH * PATCH, dtype=jnp.int32)
    row_offset = cells // PATCH - 3
    column_offset = cells % PATCH - 3

    def frame_match(inputs):
        fine_frame, coarse_frame, row_at, column_at = inputs
        fine_patch = fine_frame[row_at[:, None] + row_offset[None, :], column_at[:, None] + column_offset[None, :]].astype(jnp.float32)
        coarse_patch = coarse_frame[row_at[:, None] // 2 + row_offset[None, :], column_at[:, None] // 2 + column_offset[None, :]].astype(jnp.float32)
        fine_part = jnp.einsum('pjc,pc->pj', fine_patch, fine_feat) / math.sqrt(channels)
        coarse_part = jnp.einsum('pjc,pc->pj', coarse_patch, coarse_feat) / math.sqrt(channels)
        return jnp.concatenate([fine_part, coarse_part], axis=-1).astype(jnp.bfloat16)
    matches = lax.map(frame_match, (feature_map, pooled, pixel_row, pixel_column))
    embedding = time_embedding(window_start[0] + jnp.arange(frames, dtype=jnp.int32), features)
    projected = jnp.dot(matches.reshape(frames * points, -1), match_weight, preferred_element_type=jnp.float32)
    tokens = (projected.reshape(frames, points, features) + embedding[:, None, :]).astype(jnp.bfloat16)
    allowed = visible == 1

    def cross_one(inputs):
        frame_tokens, frame_allowed = inputs
        return transformer_block(frame_tokens[None], frame_allowed[None], layer_gains[0], joint_weight[0], output_weight[0], expand_weight[0], reduce_weight[0])[0]
    crossed = lax.map(cross_one, (tokens, allowed))
    tracked = transformer_block(jnp.transpose(crossed, (1, 0, 2)), jnp.transpose(allowed), layer_gains[1], joint_weight[1], output_weight[1], expand_weight[1], reduce_weight[1])
    tracked = jnp.transpose(tracked, (1, 0, 2))
    half_way = frames // 2
    final_rows = jnp.broadcast_to(tracked[-1:], (frames - half_way, points, features))
    return jnp.concatenate([tracked[half_way:], final_rows], axis=0)
```

```python
import math

import jax
import jax.numpy as jnp
from jax import lax
from jax.experimental import pallas as pl
from jax.experimental.pallas import tpu as pltpu
from jax.sharding import PartitionSpec as P

HEADS = 8
PATCH = 7
EPSILON = 1e-05
LANES = 128
TILE = 16
F32 = jnp.float32
BF16 = jnp.bfloat16
VMEM = pltpu.MemorySpace.VMEM
SMEM = pltpu.MemorySpace.SMEM


def normalize(values, weights):
    average = jnp.mean(values, axis=-1, keepdims=True)
    centred = values - average
    variance = jnp.mean(centred * centred, axis=-1, keepdims=True)
    return centred * lax.rsqrt(variance + EPSILON) * weights


def time_embedding(absolute, features):
    half_way = features // 2
    frequency = jnp.exp(-math.log(10000.0) * jnp.arange(half_way, dtype=F32) / half_way)
    angles = absolute.astype(F32)[:, None] * frequency[None, :]
    return jnp.concatenate([jnp.sin(angles), jnp.cos(angles)], axis=-1)


def iota(shape, axis):
    return lax.broadcasted_iota(jnp.int32, shape, axis)


def matmul(left, right):
    return jnp.dot(left, right, preferred_element_type=F32)


def matmul_nt(left, right):
    return lax.dot_general(left, right, (((1,), (1,)), ((), ())), preferred_element_type=F32)


def pack_kernel(slots, round_ref, query_ref, row_ref, column_ref, map_ref, out_ref, tiles, where_ref, fine, coarse, sems):
    me = lax.axis_index("frame")
    points = query_ref.shape[1]
    base = round_ref[0] * slots

    def tile_copy(slot, row, column):
        return pltpu.make_async_copy(
            map_ref.at[0, pl.ds(row // 2 * 2, 2), pl.ds(pl.multiple_of(column // TILE * TILE, TILE), TILE), :],
            tiles.at[slot],
            sems.at[slot],
        )

    def scan(point, found):
        mine = query_ref[0, point] == me
        slot = found - base

        @pl.when(mine & (slot >= 0) & (slot < slots))
        def _():
            row = row_ref[0, point]
            column = column_ref[0, point]
            tile_copy(slot, row, column).start()
            where_ref[slot] = row % 2 * TILE + column % TILE

        return found + mine.astype(jnp.int32)

    found = lax.fori_loop(0, points, scan, jnp.int32(0), unroll=8)
    count = jnp.clip(found - base, 0, slots)
    fine[...] = jnp.zeros_like(fine)
    coarse[...] = jnp.zeros_like(coarse)
    cell = iota((2, TILE, LANES), 0) * TILE + iota((2, TILE, LANES), 1)

    def select(slot, carry):
        tile_copy(slot, 0, 0).wait()
        at = where_ref[slot]
        tile = tiles[slot].astype(F32)
        fine[pl.ds(slot, 1), :] = jnp.sum(jnp.where(cell == at, tile, 0.0), axis=(0, 1))[None]
        near = cell % TILE // 2 == at % TILE // 2
        coarse[pl.ds(slot, 1), :] = jnp.sum(jnp.where(near, tile, 0.0), axis=(0, 1))[None] * 0.25
        return carry

    lax.fori_loop(0, count, select, 0)
    block = jnp.concatenate([fine[...], coarse[...]], axis=1).astype(BF16)
    out_ref[...] = jnp.broadcast_to(block[None], out_ref.shape)


def ranks(query_row):
    points = query_row.shape[1]
    across = jnp.broadcast_to(query_row.astype(F32), (points, points))
    down = across.T
    earlier = (across == down) & (iota((points, points), 1) < iota((points, points), 0))
    rank = jnp.sum(jnp.where(earlier, 1.0, 0.0), axis=1, keepdims=True)
    return down[:, :1].astype(jnp.int32), rank.astype(jnp.int32)


def unpack(query_row, received, slots, base):
    frame, rank = ranks(query_row)
    points, total = frame.shape[0], received.shape[0]
    inside = (rank >= base) & (rank < base + slots)
    at = jnp.where(inside, frame * slots + rank - base, -1)
    chosen = jnp.where(iota((points, total), 1) == at, 1.0, 0.0).astype(BF16)
    return matmul(chosen, received)


def attention(queries, keyset, values, permitted):
    rows, features = queries.shape
    per_head = features // HEADS
    head_of = iota((1, features), 1) // per_head
    spread = jnp.concatenate(
        [jnp.where(head_of == head, queries, 0) for head in range(HEADS)], axis=0
    )
    scores = matmul_nt(spread, keyset) * (1.0 / math.sqrt(per_head))
    outcome = None
    parts = []
    for head in range(HEADS):
        part = jnp.where(permitted, scores[head * rows : (head + 1) * rows], -1e30)
        part = jnp.exp(part - jnp.max(part, axis=-1, keepdims=True))
        parts.append((part / jnp.sum(part, axis=-1, keepdims=True)).astype(BF16))
    mixed = matmul(jnp.concatenate(parts, axis=0), values)
    for head in range(HEADS):
        term = jnp.where(head_of == head, mixed[head * rows : (head + 1) * rows], 0.0)
        outcome = term if outcome is None else outcome + term
    return outcome.astype(BF16)


def finish(stream, attended, gain, output_weight, expand_weight, reduce_weight):
    stream = stream + matmul(attended, output_weight)
    hidden = normalize(stream, gain).astype(BF16)
    widened = jax.nn.gelu(matmul(hidden, expand_weight), approximate=True).astype(BF16)
    return stream + matmul(widened, reduce_weight)


def frame_kernel(
    slots,
    row_ref,
    column_ref,
    query_ref,
    received_ref,
    extra_ref,
    map_ref,
    visible_ref,
    embedding_ref,
    match_ref,
    gains_ref,
    joint_ref,
    output_ref,
    expand_ref,
    reduce_ref,
    out_ref,
    corr,
    fine,
    coarse,
    staged,
):
    me = lax.axis_index("frame")
    points = query_ref.shape[1]
    _, height, breadth, channels = map_ref.shape
    features = match_ref.shape[1]
    devices = out_ref.shape[0]
    received = received_ref[...].reshape(devices * slots, 2 * channels)
    anchors = (unpack(query_ref[...], received, slots, 0) + extra_ref[...].astype(F32)).astype(BF16)
    lane = iota((1, LANES), 1)
    feats = []
    for start in range(0, points, LANES):
        both = jnp.concatenate(
            [anchors[start : start + LANES, :channels], anchors[start : start + LANES, channels:]], axis=0
        )

        def correlate(pair, carry):
            cells = map_ref[0, pl.ds(pair * 2, 2)].reshape(2 * breadth, channels)
            product = matmul_nt(both, cells)
            at = pl.multiple_of(pair * 4 * LANES, 4 * LANES)
            corr[pl.ds(at, 2 * LANES), :] = product[:, :breadth]
            corr[pl.ds(at + 2 * LANES, 2 * LANES), :] = product[:, breadth:]
            return carry

        lax.fori_loop(0, height // 2, correlate, 0, unroll=2)

        def extract(point, carry):
            row = row_ref[0, start + point]
            column = column_ref[0, start + point]
            window = corr[pl.ds((row - 3) * 2 * LANES + point, 8, stride=2 * LANES), :]
            fine[pl.ds(pl.multiple_of(point * 8, 8), 8), :] = pltpu.roll(window, LANES + 3 - column, 1)
            top = row // 2 * 2 - 6
            at = top * 2 * LANES + LANES + point
            pairs = (
                corr[pl.ds(at, 8, stride=4 * LANES), :]
                + corr[pl.ds(at + 2 * LANES, 8, stride=4 * LANES), :]
            )
            coarse[pl.ds(pl.multiple_of(point * 8, 8), 8), :] = pltpu.roll(
                pairs, LANES + 6 - column // 2 * 2, 1
            )
            return carry

        lax.fori_loop(0, LANES, extract, 0, unroll=8)

        def merged(ref):
            result = None
            for k in range(PATCH):
                part = ref[pl.ds(k, LANES, stride=8), :]
                result = part if k == 0 else jnp.where(lane // TILE == k, pltpu.roll(part, k * TILE, 1), result)
            return result

        scale = 1.0 / math.sqrt(channels)
        level_0 = merged(fine) * scale
        level_1 = merged(coarse)
        level_1 = (level_1 + pltpu.roll(level_1, LANES - 1, 1)) * (0.25 * scale)
        feats.append(jnp.concatenate([level_0, level_1], axis=1).astype(BF16))
    matches = jnp.concatenate(feats, axis=0)
    cells = match_ref.shape[0]
    place = iota((2 * LANES, cells), 0)
    level = place // LANES
    k, m = place % LANES // TILE, place % TILE
    m_at = jnp.where(level == 0, m, m // 2)
    valid = (k < PATCH) & (m_at < PATCH) & ((level == 0) | (m % 2 == 0))
    wanted = jnp.where(valid, level * PATCH * PATCH + k * PATCH + m_at, -1)
    pick = jnp.where(iota((2 * LANES, cells), 1) == wanted, 1.0, 0.0).astype(BF16)
    weights = matmul(pick, match_ref[...]).astype(BF16)
    tokens = (matmul(matches, weights) + embedding_ref[...]).astype(BF16)

    stream = tokens.astype(F32)
    hidden = normalize(stream, gains_ref[0, 0:1, :]).astype(BF16)
    projected = matmul(hidden, joint_ref[0]).astype(BF16)
    allowed = visible_ref[pl.ds(me, 1), :] == 1
    permitted = allowed | (iota((points, points), 0) == iota((points, points), 1))
    attended = attention(
        projected[:, :features], projected[:, features : 2 * features], projected[:, 2 * features :], permitted
    )
    crossed = finish(stream, attended, gains_ref[0, 1:2, :], output_ref[0], expand_ref[0], reduce_ref[0])
    pad_rows = out_ref.shape[1]
    chunks = features // LANES
    for i in range(points // devices):
        for c in range(chunks):
            staged[pl.ds(i * chunks + c, devices, stride=pad_rows), :] = crossed[
                i * devices : (i + 1) * devices, c * LANES : (c + 1) * LANES
            ]
    out_ref[...] = staged[...].astype(BF16).reshape(out_ref.shape)


def track_kernel(
    per_device,
    received_ref,
    visible_ref,
    gains_ref,
    joint_ref,
    output_ref,
    expand_ref,
    reduce_ref,
    out_ref,
    staged,
):
    me = lax.axis_index("frame")
    length, pad_rows, _ = received_ref.shape
    features = output_ref.shape[1]
    chunks = features // LANES
    points = visible_ref.shape[1]
    devices = out_ref.shape[0]
    half_way = length // 2
    staged[...] = received_ref[...].reshape(length * pad_rows, LANES).astype(F32)
    stream = jnp.concatenate(
        [
            jnp.concatenate(
                [staged[pl.ds(i * chunks + c, length, stride=pad_rows), :] for c in range(chunks)], axis=1
            )
            for i in range(per_device)
        ],
        axis=0,
    )
    total = per_device * length
    hidden = normalize(stream, gains_ref[1, 0:1, :]).astype(BF16)
    projected = matmul(hidden, joint_ref[1]).astype(BF16)

    def later(array):
        return jnp.concatenate(
            [array[i * length + half_way : (i + 1) * length] for i in range(per_device)], axis=0
        )

    rest = length - half_way
    lane = iota((points, total), 1)
    pick = jnp.where(iota((points, total), 0) == lane // length * devices + me, 1.0, 0.0).astype(BF16)
    seen = matmul(jnp.where(visible_ref[...] == 1, 1.0, 0.0).astype(BF16), pick)
    seen = jnp.where(iota((length, total), 1) % length == iota((length, total), 0), seen, 0.0)
    allowed = jnp.sum(seen, axis=0, keepdims=True) > 0.5
    query_at = iota((per_device * rest, total), 0)
    key_at = iota((per_device * rest, total), 1)
    same_point = query_at // rest == key_at // length
    same_frame = query_at % rest + half_way == key_at % length
    permitted = same_point & (allowed | same_frame)
    attended = attention(
        later(projected[:, :features]),
        projected[:, features : 2 * features],
        projected[:, 2 * features :],
        permitted,
    )
    tracked = finish(later(stream), attended, gains_ref[1, 1:2, :], output_ref[1], expand_ref[1], reduce_ref[1])
    for i in range(per_device):
        for c in range(chunks):
            piece = tracked[i * rest : (i + 1) * rest, c * LANES : (c + 1) * LANES]
            at = i * chunks + c
            staged[pl.ds(at, rest, stride=pad_rows), :] = piece
            staged[pl.ds(rest * pad_rows + at, half_way, stride=pad_rows), :] = jnp.broadcast_to(
                piece[rest - 1 :], (half_way, LANES)
            )
    out_ref[...] = staged[...].astype(BF16).reshape(out_ref.shape)


def layout_kernel(received_ref, out_ref, staged):
    devices, pad_rows, _ = received_ref.shape
    _, points, features = out_ref.shape
    chunks = features // LANES
    staged[...] = received_ref[...].reshape(devices * pad_rows, LANES).astype(F32)
    for i in range(points // devices):
        for c in range(chunks):
            out_ref[0, i * devices : (i + 1) * devices, c * LANES : (c + 1) * LANES] = staged[
                pl.ds(i * chunks + c, devices, stride=pad_rows), :
            ].astype(BF16)


def shards(
    feature_map,
    pixel_row,
    pixel_column,
    query_frame,
    visible,
    window_start,
    match_weight,
    layer_gains,
    joint_weight,
    output_weight,
    expand_weight,
    reduce_weight,
):
    frames, height, breadth, channels = feature_map.shape
    points = query_frame.shape[0]
    features = match_weight.shape[1]
    devices = lax.axis_size("frame")
    position = lax.axis_index("frame")
    per_device = points // devices
    slots = TILE * -(-4 * per_device // TILE)
    pad_rows = TILE * -(-per_device * (features // LANES) // TILE)
    query_row = query_frame.reshape(1, points)
    vmem = pl.BlockSpec(memory_space=VMEM)
    smem = pl.BlockSpec(memory_space=SMEM)

    pack = pl.pallas_call(
        lambda *refs: pack_kernel(slots, *refs),
        out_shape=jax.ShapeDtypeStruct((devices, slots, 2 * channels), BF16),
        in_specs=[smem, smem, smem, smem, pl.BlockSpec(memory_space=pl.ANY)],
        out_specs=vmem,
        scratch_shapes=[
            pltpu.VMEM((slots, 2, TILE, LANES), BF16),
            pltpu.SMEM((slots,), jnp.int32),
            pltpu.VMEM((slots, LANES), F32),
            pltpu.VMEM((slots, LANES), F32),
            pltpu.SemaphoreType.DMA((slots,)),
        ],
        name="pack",
    )

    def exchange(block):
        return lax.all_to_all(block, "frame", split_axis=0, concat_axis=0, tiled=True)

    def send_round(which):
        return exchange(pack(which.reshape(1), query_row, pixel_row, pixel_column, feature_map))

    received = send_round(jnp.int32(0))
    load = jnp.sum(query_frame[:, None] == jnp.arange(devices)[None, :], axis=0)
    rounds = lax.pmax((jnp.max(load) + slots - 1) // slots, "groups")

    def next_round(state):
        which, extra = state
        again = send_round(which).reshape(devices * slots, 2 * channels)
        return which + 1, extra + unpack(query_row, again, slots, which * slots).astype(BF16)

    _, extra = lax.while_loop(
        lambda state: state[0] < rounds, next_round, (jnp.int32(1), jnp.zeros((points, 2 * channels), BF16))
    )
    frame_ids = position * frames + jnp.arange(frames, dtype=jnp.int32)
    embedding = time_embedding(window_start[0] + frame_ids, features)
    crossed = pl.pallas_call(
        lambda *refs: frame_kernel(slots, *refs),
        out_shape=jax.ShapeDtypeStruct((devices, pad_rows, LANES), BF16),
        in_specs=[smem, smem] + [vmem] * 12,
        out_specs=vmem,
        scratch_shapes=[
            pltpu.VMEM(((height + 2) * 2 * LANES, LANES), F32),
            pltpu.VMEM((8 * LANES, LANES), F32),
            pltpu.VMEM((8 * LANES, LANES), F32),
            pltpu.VMEM((devices * pad_rows, LANES), F32),
        ],
        name="frame_block",
    )(
        pixel_row,
        pixel_column,
        query_row,
        received,
        extra,
        feature_map,
        visible,
        embedding,
        match_weight,
        layer_gains,
        joint_weight,
        output_weight,
        expand_weight,
        reduce_weight,
    )
    by_track = exchange(crossed)
    tracked = pl.pallas_call(
        lambda *refs: track_kernel(per_device, *refs),
        out_shape=jax.ShapeDtypeStruct((devices, pad_rows, LANES), BF16),
        in_specs=[vmem] * 7,
        out_specs=vmem,
        scratch_shapes=[pltpu.VMEM((devices * pad_rows, LANES), F32)],
        name="track_block",
    )(by_track, visible, layer_gains, joint_weight, output_weight, expand_weight, reduce_weight)
    arrived = exchange(tracked)
    return pl.pallas_call(
        layout_kernel,
        out_shape=jax.ShapeDtypeStruct((1, points, features), BF16),
        in_specs=[vmem],
        out_specs=vmem,
        scratch_shapes=[pltpu.VMEM((devices * pad_rows, LANES), F32)],
        name="layout",
    )(arrived)


def solution(mesh):
    placed = (
        P("frame", "groups", None, None),
        P("frame", "groups"),
        P("frame", "groups"),
        P("groups"),
        P(None, "groups"),
        P("groups"),
        P(),
        P(),
        P(),
        P(),
        P(),
        P(),
    )
    return jax.shard_map(
        shards, mesh=mesh, in_specs=placed, out_specs=P("frame", "groups", None), check_vma=False
    )
```

```python
import math

import jax
import jax.numpy as jnp
from jax import lax
from jax.experimental import pallas as pl
from jax.experimental.pallas import tpu as pltpu
from jax.sharding import PartitionSpec as P

HEADS = 8
PATCH = 7
EPSILON = 1e-05
LANES = 128
TILE = 16
SPAN = 64
MIB = 1 << 20
F32 = jnp.float32
BF16 = jnp.bfloat16
VMEM = pltpu.MemorySpace.VMEM
SMEM = pltpu.MemorySpace.SMEM


def normalize(values, weights):
    average = jnp.mean(values, axis=-1, keepdims=True)
    centred = values - average
    variance = jnp.mean(centred * centred, axis=-1, keepdims=True)
    return centred * lax.rsqrt(variance + EPSILON) * weights


def iota(shape, axis):
    return lax.broadcasted_iota(jnp.int32, shape, axis)


def matmul(left, right):
    return jnp.dot(left, right, preferred_element_type=F32)


def matmul_nt(left, right):
    return lax.dot_general(left, right, (((1,), (1,)), ((), ())), preferred_element_type=F32)


def pack(slots, base, query, row, column, copies, cells, out_ref):
    me = lax.axis_index("frame")
    points = query.shape[1]
    chunks, depth, breadth, channels = cells.shape
    mine = query == me
    before = jnp.where(iota((points, points), 0) < iota((points, points), 1), 1.0, 0.0).astype(BF16)
    rank = matmul(jnp.broadcast_to(jnp.where(mine, 1.0, 0.0), (8, points)).astype(BF16), before)[:1]
    slot = jnp.where(mine, rank.astype(jnp.int32) - base, -1)
    rows = block_rows(slots)
    line = iota((rows, points), 0)
    held = jnp.where(line < slots, line, line - slots) == jnp.where(slot < slots, slot, -1)

    def gathered(values):
        return jnp.sum(jnp.where(held, values + 1, 0).astype(F32), axis=1, keepdims=True).astype(jnp.int32) - 1

    fine_at = gathered(row * breadth + column)
    coarse_at = gathered((row >> 1) * (breadth // 2) + (column >> 1))
    is_fine = iota((rows, 1), 0) < slots
    wanted = jnp.where(is_fine, fine_at, coarse_at)
    size = depth * breadth
    place = iota((1, size), 1)
    coarse_place = (place // breadth >> 1) * (breadth // 2) + (place % breadth >> 1)
    both_places = jnp.where(is_fine, place, coarse_place)
    weight = jnp.where(is_fine, 1.0, 0.25)
    total = None
    for chunk in range(chunks):
        start = jnp.where(is_fine, chunk * size, chunk * size // 4)
        chosen = jnp.where(both_places == wanted - start, weight, 0.0).astype(BF16)
        copies[chunk].wait()
        part = matmul(chosen, cells[chunk].reshape(size, channels))
        total = part if total is None else total + part
    twice = jnp.concatenate([total, total], axis=0).astype(BF16)
    for pair in range(out_ref.shape[0] // (2 * rows)):
        out_ref[pair * 2 * rows : (pair + 1) * 2 * rows, :] = twice


def map_copies(map_ref, cells, sems):
    chunks, depth, _, _ = cells.shape
    copies = [
        pltpu.make_async_copy(map_ref.at[0, pl.ds(chunk * depth, depth)], cells.at[chunk], sems.at[chunk])
        for chunk in range(chunks)
    ]
    for copy in copies:
        copy.start()
    return copies


def pack_again_kernel(slots, round_ref, query_ref, row_ref, column_ref, map_ref, out_ref, cells, sems):
    copies = map_copies(map_ref, cells, sems)
    pack(slots, round_ref[0] * slots, query_ref[...], row_ref[...], column_ref[...], copies, cells, out_ref)


def unpack_again_kernel(slots, devices, round_ref, query_ref, received_ref, before_ref, out_ref):
    chosen = choose(query_ref[...], devices, slots, round_ref[0] * slots)
    out_ref[...] = before_ref[...] + matmul(chosen, received_ref[...]).astype(BF16)


def block_rows(slots):
    return 8 * -(-2 * slots // 8)


def choose(query_row, devices, slots, base):
    points = query_row.shape[1]
    across = jnp.broadcast_to(query_row.astype(F32), (points, points))
    down = across.T
    earlier = (across == down) & (iota((points, points), 1) < iota((points, points), 0))
    rank = jnp.sum(jnp.where(earlier, 1.0, 0.0), axis=1, keepdims=True).astype(jnp.int32)
    frame = down[:, :1].astype(jnp.int32)
    rows = block_rows(slots)
    inside = (rank >= base) & (rank < base + slots)
    fine_at = jnp.where(inside, frame * rows + rank - base, -1)
    coarse_at = jnp.where(inside, frame * rows + slots + rank - base, -1)
    place = iota((points, devices * rows), 1)
    chosen = [jnp.where(place == at, 1.0, 0.0).astype(BF16) for at in (fine_at, coarse_at)]
    return jnp.concatenate(chosen, axis=0)


def prepare_kernel(
    slots,
    row_ref,
    column_ref,
    window_ref,
    query_ref,
    row_line_ref,
    column_line_ref,
    match_ref,
    map_ref,
    packed_ref,
    rounds_ref,
    chosen_ref,
    fine_ref,
    coarse_ref,
    spread_ref,
    embedding_ref,
    cells,
    fine_map,
    coarse_map,
    match,
    sems,
    match_sem,
):
    match_copy = pltpu.make_async_copy(match_ref, match, match_sem)
    match_copy.start()
    copies = map_copies(map_ref, cells, sems)
    me = lax.axis_index("frame")
    points = query_ref.shape[1]
    _, height, breadth, channels = map_ref.shape
    depth = cells.shape[1]
    half = breadth // 2
    rows = block_rows(slots)
    devices = packed_ref.shape[0] // rows
    query = query_ref[...]
    chosen_ref[...] = choose(query, devices, slots, 0)
    there = jnp.where(iota((devices, points), 0) == query, 1.0, 0.0)
    load = jnp.max(jnp.sum(there, axis=1, keepdims=True)).astype(jnp.int32)
    rounds_ref[0] = (load + slots - 1) // slots
    place = iota((2 * SPAN, match_ref.shape[0]), 0)
    level, k, m = place // SPAN, place % SPAN // 8, place % 8
    wanted = jnp.where((k < PATCH) & (m < PATCH), (level * PATCH + k) * PATCH + m, -1)
    pick = jnp.where(iota(place.shape, 1) == wanted, 1.0, 0.0).astype(BF16)
    match_copy.wait()
    spread_ref[...] = matmul(pick, match[...]).astype(BF16)
    features = embedding_ref.shape[1]
    feature = iota((1, features), 1)
    of_sine = feature < features // 2
    step = jnp.where(of_sine, feature, feature - features // 2).astype(F32)
    angle = (window_ref[0] + me).astype(F32) * jnp.exp(-math.log(10000.0) * step / (features // 2))
    embedding_ref[...] = jnp.where(of_sine, jnp.sin(angle), jnp.cos(angle))
    pack(slots, 0, query, row_line_ref[...], column_line_ref[...], copies, cells, packed_ref)
    pool = jnp.where(
        iota((half, 2 * breadth), 1) % breadth // 2 == iota((half, 2 * breadth), 0), 0.25, 0.0
    ).astype(BF16)
    coarse_map[pl.ds(height // 2 * half, 8), :] = jnp.zeros((8, channels), F32)

    def convert(pair, carry):
        both = cells.reshape(height * breadth, channels)[
            pl.ds(pl.multiple_of(pair * 2 * breadth, 2 * breadth), 2 * breadth), :
        ]
        fine_map[pl.ds(pl.multiple_of(pair * 2 * breadth, 2 * breadth), 2 * breadth), :] = both.astype(F32)
        coarse_map[pl.ds(pl.multiple_of(pair * half, half), half), :] = matmul(pool, both).astype(BF16).astype(F32)
        return carry

    lax.fori_loop(0, height // 2, convert, 0, unroll=4)
    blank = jnp.zeros((8, channels), F32)

    def gather(point, carry):
        row, column = row_ref[0, point], column_ref[0, point]
        for ref, out, wide, at in (
            (fine_map, fine_ref, breadth, row * breadth + column - (3 * breadth + 3)),
            (coarse_map, coarse_ref, half, (row >> 1) * half + (column >> 1) - (3 * half + 3)),
        ):
            window = ref.at[pl.ds(at, 6 * wide + 8), :]
            target = out.at[pl.ds(pl.multiple_of(point * SPAN, SPAN), SPAN), :]
            lines = [window[k * wide : k * wide + 8, :] for k in range(PATCH)] + [blank]
            for t in range(4):
                target[t * TILE : (t + 1) * TILE, :] = jnp.concatenate(lines[2 * t : 2 * t + 2], axis=0).astype(BF16)
        return carry

    lax.fori_loop(0, points, gather, 0, unroll=8)


def attention(queries, keyset, values, permitted):
    rows, features = queries.shape
    per_head = features // HEADS
    head_of = iota((1, features), 1) // per_head
    spread = jnp.concatenate(
        [jnp.where(head_of == head, queries, 0) for head in range(HEADS)], axis=0
    )
    scores = matmul_nt(spread, keyset) * (1.0 / math.sqrt(per_head))
    outcome = None
    parts = []
    for head in range(HEADS):
        part = jnp.where(permitted, scores[head * rows : (head + 1) * rows], -1e30)
        part = jnp.exp(part - jnp.max(part, axis=-1, keepdims=True))
        parts.append((part / jnp.sum(part, axis=-1, keepdims=True)).astype(BF16))
    mixed = matmul(jnp.concatenate(parts, axis=0), values)
    for head in range(HEADS):
        term = jnp.where(head_of == head, mixed[head * rows : (head + 1) * rows], 0.0)
        outcome = term if outcome is None else outcome + term
    return outcome.astype(BF16)


def finish(stream, attended, gain, output_weight, expand_weight, reduce_weight):
    stream = stream + matmul(attended, output_weight)
    hidden = normalize(stream, gain).astype(BF16)
    widened = jax.nn.gelu(matmul(hidden, expand_weight), approximate=True).astype(BF16)
    return stream + matmul(widened, reduce_weight)


def frame_kernel(
    extra_ref,
    received_ref,
    chosen_ref,
    fine_ref,
    coarse_ref,
    spread_ref,
    embedding_ref,
    visible_ref,
    gains_ref,
    joint_ref,
    output_ref,
    expand_ref,
    reduce_ref,
    out_ref,
    staged,
):
    me = lax.axis_index("frame")
    points = visible_ref.shape[1]
    channels = received_ref.shape[1]
    features = spread_ref.shape[1]
    devices, pad_rows, _ = out_ref.shape
    anchors = matmul(chosen_ref[...], received_ref[...]).astype(BF16)
    if extra_ref is not None:
        anchors = anchors + extra_ref[...]
    line, lane = iota((8, LANES), 0), iota((8, LANES), 1)
    rows = []
    for start in range(0, points, TILE):
        levels = []
        for level, ref in enumerate((fine_ref, coarse_ref)):
            some = anchors[level * points + start : level * points + start + TILE]
            levels.append(matmul_nt(some, ref[start * SPAN : (start + TILE) * SPAN, :]))
        for part in range(2):
            sides = []
            for level, scores in enumerate(levels):
                own = scores[part * 8 : part * 8 + 8, part * 8 * SPAN : (part + 1) * 8 * SPAN]
                kept = own[:, :LANES]
                for index in range(1, 4):
                    kept = jnp.where(line // 2 == index, own[:, index * LANES : (index + 1) * LANES], kept)
                sides.append(jnp.where(line % 2 == level, kept, pltpu.roll(kept, SPAN, 1)))
            rows.append(jnp.where(lane < SPAN, sides[0], sides[1]))
    matches = (jnp.concatenate(rows, axis=0) * (1.0 / math.sqrt(channels))).astype(BF16)
    tokens = (matmul(matches, spread_ref[...]) + embedding_ref[...]).astype(BF16)

    stream = tokens.astype(F32)
    hidden = normalize(stream, gains_ref[0, 0:1, :]).astype(BF16)
    projected = matmul(hidden, joint_ref[0]).astype(BF16)
    allowed = visible_ref[pl.ds(me, 1), :] == 1
    permitted = allowed | (iota((points, points), 0) == iota((points, points), 1))
    attended = attention(
        projected[:, :features], projected[:, features : 2 * features], projected[:, 2 * features :], permitted
    )
    crossed = finish(stream, attended, gains_ref[0, 1:2, :], output_ref[0], expand_ref[0], reduce_ref[0])
    chunks = features // LANES
    for i in range(points // devices):
        for c in range(chunks):
            staged[pl.ds(i * chunks + c, devices, stride=pad_rows), :] = crossed[
                i * devices : (i + 1) * devices, c * LANES : (c + 1) * LANES
            ]
    out_ref[...] = staged[...].astype(BF16).reshape(out_ref.shape)


def track_kernel(
    per_device,
    received_ref,
    visible_ref,
    gains_ref,
    joint_ref,
    output_ref,
    expand_ref,
    reduce_ref,
    out_ref,
    staged,
):
    me = lax.axis_index("frame")
    length, pad_rows, _ = received_ref.shape
    features = output_ref.shape[1]
    chunks = features // LANES
    points = visible_ref.shape[1]
    devices = out_ref.shape[0]
    half_way = length // 2
    staged[...] = received_ref[...].reshape(length * pad_rows, LANES).astype(F32)
    stream = jnp.concatenate(
        [
            jnp.concatenate(
                [staged[pl.ds(i * chunks + c, length, stride=pad_rows), :] for c in range(chunks)], axis=1
            )
            for i in range(per_device)
        ],
        axis=0,
    )
    total = per_device * length
    hidden = normalize(stream, gains_ref[1, 0:1, :]).astype(BF16)
    projected = matmul(hidden, joint_ref[1]).astype(BF16)

    def later(array):
        return jnp.concatenate(
            [array[i * length + half_way : (i + 1) * length] for i in range(per_device)], axis=0
        )

    rest = length - half_way
    lane = iota((points, total), 1)
    pick = jnp.where(iota((points, total), 0) == lane // length * devices + me, 1.0, 0.0).astype(BF16)
    seen = matmul(jnp.where(visible_ref[...] == 1, 1.0, 0.0).astype(BF16), pick)
    seen = jnp.where(iota((length, total), 1) % length == iota((length, total), 0), seen, 0.0)
    allowed = jnp.sum(seen, axis=0, keepdims=True) > 0.5
    query_at = iota((per_device * rest, total), 0)
    key_at = iota((per_device * rest, total), 1)
    same_point = query_at // rest == key_at // length
    same_frame = query_at % rest + half_way == key_at % length
    permitted = same_point & (allowed | same_frame)
    attended = attention(
        later(projected[:, :features]),
        projected[:, features : 2 * features],
        projected[:, 2 * features :],
        permitted,
    )
    tracked = finish(later(stream), attended, gains_ref[1, 1:2, :], output_ref[1], expand_ref[1], reduce_ref[1])
    for i in range(per_device):
        for c in range(chunks):
            piece = tracked[i * rest : (i + 1) * rest, c * LANES : (c + 1) * LANES]
            at = i * chunks + c
            staged[pl.ds(at, rest, stride=pad_rows), :] = piece
            staged[pl.ds(rest * pad_rows + at, half_way, stride=pad_rows), :] = jnp.broadcast_to(
                piece[rest - 1 :], (half_way, LANES)
            )
    out_ref[...] = staged[...].astype(BF16).reshape(out_ref.shape)


def layout_kernel(received_ref, out_ref, staged):
    devices, pad_rows, _ = received_ref.shape
    _, points, features = out_ref.shape
    chunks = features // LANES
    staged[...] = received_ref[...].reshape(devices * pad_rows, LANES).astype(F32)
    for i in range(points // devices):
        for c in range(chunks):
            out_ref[0, i * devices : (i + 1) * devices, c * LANES : (c + 1) * LANES] = staged[
                pl.ds(i * chunks + c, devices, stride=pad_rows), :
            ].astype(BF16)


def exchange(block):
    return lax.all_to_all(block, "frame", split_axis=0, concat_axis=0, tiled=True)


def step(
    further,
    feature_map,
    pixel_row,
    pixel_column,
    query_frame,
    visible,
    window_start,
    match_weight,
    layer_gains,
    *weights,
):
    _, height, breadth, channels = feature_map.shape
    points = query_frame.shape[0]
    features = match_weight.shape[1]
    devices = lax.axis_size("frame")
    per_device = points // devices
    slots = 3 * per_device
    rows = block_rows(slots)
    pad_rows = TILE * -(-per_device * (features // LANES) // TILE)
    query_row = query_frame.reshape(1, points)
    vmem = pl.BlockSpec(memory_space=VMEM)
    smem = pl.BlockSpec(memory_space=SMEM)
    here = pl.BlockSpec(memory_space=pltpu.MemorySpace.HBM)
    chunks = 8
    map_scratch = pltpu.VMEM((chunks, height // chunks, breadth, channels), BF16)
    map_sems = pltpu.SemaphoreType.DMA((chunks,))
    block = jax.ShapeDtypeStruct((devices * rows, channels), BF16)

    packed, rounds, *prepared = pl.pallas_call(
        lambda *refs: prepare_kernel(slots, *refs),
        out_shape=[
            block,
            jax.ShapeDtypeStruct((1,), jnp.int32),
            jax.ShapeDtypeStruct((2 * points, devices * rows), BF16),
            jax.ShapeDtypeStruct((points * SPAN, channels), BF16),
            jax.ShapeDtypeStruct((points * SPAN, channels), BF16),
            jax.ShapeDtypeStruct((2 * SPAN, features), BF16),
            jax.ShapeDtypeStruct((1, features), F32),
        ],
        in_specs=[smem, smem, smem, vmem, vmem, vmem, here, here],
        out_specs=[vmem, smem] + [vmem] * 5,
        scratch_shapes=[
            map_scratch,
            pltpu.VMEM((height * breadth, channels), F32),
            pltpu.VMEM((height * breadth // 4 + 8, channels), F32),
            pltpu.VMEM(match_weight.shape, BF16),
            map_sems,
            pltpu.SemaphoreType.DMA,
        ],
        compiler_params=pltpu.CompilerParams(vmem_limit_bytes=(16 + points // 16) * MIB),
        name="prepare",
    )(
        pixel_row,
        pixel_column,
        window_start,
        query_row,
        pixel_row,
        pixel_column,
        match_weight,
        feature_map,
    )
    rounds = rounds.reshape(())
    received = exchange(packed)
    extra = ()
    if further:

        def next_round(state):
            which, extra = state
            again = pl.pallas_call(
                lambda *refs: pack_again_kernel(slots, *refs),
                out_shape=block,
                in_specs=[smem, vmem, vmem, vmem, here],
                out_specs=vmem,
                scratch_shapes=[map_scratch, map_sems],
                compiler_params=pltpu.CompilerParams(vmem_limit_bytes=8 * MIB),
                name="pack_again",
            )(which.reshape(1), query_row, pixel_row, pixel_column, feature_map)
            extra = pl.pallas_call(
                lambda *refs: unpack_again_kernel(slots, devices, *refs),
                out_shape=jax.ShapeDtypeStruct(extra.shape, BF16),
                in_specs=[smem, vmem, vmem, vmem],
                out_specs=vmem,
                compiler_params=pltpu.CompilerParams(vmem_limit_bytes=(4 + points // 16) * MIB),
                name="unpack_again",
            )(which.reshape(1), query_row, exchange(again), extra)
            return which + 1, extra

        received, rounds = lax.optimization_barrier((received, lax.pmax(rounds, "groups")))
        start = (jnp.int32(1), jnp.zeros((2 * points, channels), BF16))
        extra = lax.while_loop(lambda state: state[0] < rounds, next_round, start)[1:]
    crossed = pl.pallas_call(
        frame_kernel if further else lambda *refs: frame_kernel(None, *refs),
        out_shape=jax.ShapeDtypeStruct((devices, pad_rows, LANES), BF16),
        in_specs=[vmem] * (12 + len(extra)),
        out_specs=vmem,
        scratch_shapes=[pltpu.VMEM((devices * pad_rows, LANES), F32)],
        compiler_params=pltpu.CompilerParams(vmem_limit_bytes=(8 + points // 16) * MIB),
        name="frame_block",
    )(*extra, received, *prepared, visible, layer_gains, *weights)
    by_track = exchange(crossed)
    tracked = pl.pallas_call(
        lambda *refs: track_kernel(per_device, *refs),
        out_shape=jax.ShapeDtypeStruct((devices, pad_rows, LANES), BF16),
        in_specs=[vmem] * 7,
        out_specs=vmem,
        scratch_shapes=[pltpu.VMEM((devices * pad_rows, LANES), F32)],
        compiler_params=pltpu.CompilerParams(vmem_limit_bytes=(4 + points // 16) * MIB),
        name="track_block",
    )(by_track, visible, layer_gains, *weights)
    arrived = exchange(tracked)
    handed = pl.pallas_call(
        layout_kernel,
        out_shape=jax.ShapeDtypeStruct((1, points, features), BF16),
        in_specs=[vmem],
        out_specs=vmem,
        scratch_shapes=[pltpu.VMEM((devices * pad_rows, LANES), F32)],
        compiler_params=pltpu.CompilerParams(vmem_limit_bytes=4 * MIB),
        name="layout",
    )(arrived)
    return rounds, handed


def shards(*arrays):
    rounds, handed = step(False, *arrays)

    def again(state):
        rounds, _ = state
        return jnp.int32(1), step(True, *lax.optimization_barrier((rounds,) + arrays)[1:])[1]

    return lax.while_loop(lambda state: state[0] > 1, again, (lax.pmax(rounds, "groups"), handed))[1]


def solution(mesh):
    placed = (
        P("frame", "groups", None, None),
        P("frame", "groups"),
        P("frame", "groups"),
        P("groups"),
        P(None, "groups"),
        P("groups"),
        P(),
        P(),
        P(),
        P(),
        P(),
        P(),
    )
    return jax.shard_map(
        shards, mesh=mesh, in_specs=placed, out_specs=P("frame", "groups", None), check_vma=False
    )
```

```python
import math

import jax
import jax.numpy as jnp
from jax import lax
from jax.experimental import pallas as pl
from jax.experimental.pallas import tpu as pltpu
from jax.sharding import PartitionSpec as P

HEADS = 8
PATCH = 7
EPSILON = 1e-05
LANES = 128
TILE = 16
SPAN = 64
MIB = 1 << 20
F32 = jnp.float32
BF16 = jnp.bfloat16
VMEM = pltpu.MemorySpace.VMEM
SMEM = pltpu.MemorySpace.SMEM


def normalize(values, weights):
    average = jnp.mean(values, axis=-1, keepdims=True)
    centred = values - average
    variance = jnp.mean(centred * centred, axis=-1, keepdims=True)
    return centred * lax.rsqrt(variance + EPSILON) * weights


def iota(shape, axis):
    return lax.broadcasted_iota(jnp.int32, shape, axis)


def matmul(left, right):
    return jnp.dot(left, right, preferred_element_type=F32)


def matmul_nt(left, right):
    return lax.dot_general(left, right, (((1,), (1,)), ((), ())), preferred_element_type=F32)


def slot_cells(slots, base, query, row, column, breadth):
    me = lax.axis_index("frame")
    points = query.shape[1]
    mine = query == me
    before = jnp.where(iota((points, points), 0) < iota((points, points), 1), 1.0, 0.0).astype(BF16)
    rank = matmul(jnp.broadcast_to(jnp.where(mine, 1.0, 0.0), (8, points)).astype(BF16), before)[:1]
    slot = jnp.where(mine, rank.astype(jnp.int32) - base, -1)
    rows = TILE * -(-block_rows(slots) // TILE)
    line = iota((rows, points), 0)
    held = jnp.where(line < slots, line, line - slots) == jnp.where(slot < slots, slot, -1)

    def gathered(values):
        return jnp.sum(jnp.where(held, values + 1, 0).astype(F32), axis=1, keepdims=True).astype(jnp.int32) - 1

    is_fine = iota((rows, 1), 0) < slots
    fine_at = gathered(row * breadth + column)
    coarse_at = gathered((row >> 1) * (breadth // 2) + (column >> 1))
    return is_fine, jnp.where(is_fine, fine_at, coarse_at)


def slot_weights(is_fine, wanted, pair, breadth):
    lane = iota((1, 2 * breadth), 1)
    column = jnp.where(lane < breadth, lane, lane - breadth)
    places = jnp.where(is_fine, lane, column >> 1)
    start = jnp.where(is_fine, pair * (2 * breadth), pair * (breadth // 2))
    return jnp.where(places == wanted - start, jnp.where(is_fine, 1.0, 0.25), 0.0).astype(BF16)


def send_block(total, rows, out_ref):
    block = total[:rows]
    twice = jnp.concatenate([block, block], axis=0).astype(BF16)
    for pair in range(out_ref.shape[0] // (2 * rows)):
        out_ref[pair * 2 * rows : (pair + 1) * 2 * rows, :] = twice


def map_copy(map_ref, cells, sems, chunk):
    depth = cells.shape[1]
    return pltpu.make_async_copy(map_ref.at[0, pl.ds(chunk * depth, depth)], cells.at[chunk], sems.at[chunk])


def each_pair(map_ref, cells, sems, body, carry):
    chunks, depth, breadth, channels = cells.shape

    def walk(chunk, carry):
        map_copy(map_ref, cells, sems, chunk).wait()
        for inner in range(depth // 2):
            both = cells[chunk, 2 * inner : 2 * inner + 2].reshape(2 * breadth, channels)
            carry = body(chunk * (depth // 2) + inner, both, carry)
        return carry

    return lax.fori_loop(0, chunks, walk, carry)


def pack_again_kernel(slots, round_ref, query_ref, row_ref, column_ref, map_ref, out_ref, cells, sems):
    chunks, _, breadth, channels = cells.shape
    for chunk in range(chunks):
        map_copy(map_ref, cells, sems, chunk).start()
    is_fine, wanted = slot_cells(slots, round_ref[0] * slots, query_ref[...], row_ref[...], column_ref[...], breadth)

    def body(pair, both, total):
        return total + matmul(slot_weights(is_fine, wanted, pair, breadth), both)

    total = each_pair(map_ref, cells, sems, body, jnp.zeros((wanted.shape[0], channels), F32))
    send_block(total, block_rows(slots), out_ref)


def unpack_again_kernel(slots, devices, round_ref, query_ref, received_ref, before_ref, out_ref):
    chosen = choose(query_ref[...], devices, slots, round_ref[0] * slots)
    out_ref[...] = before_ref[...] + matmul(chosen, received_ref[...]).astype(BF16)


def block_rows(slots):
    return 8 * -(-2 * slots // 8)


def choose(query_row, devices, slots, base):
    points = query_row.shape[1]
    across = jnp.broadcast_to(query_row.astype(F32), (points, points))
    down = across.T
    earlier = (across == down) & (iota((points, points), 1) < iota((points, points), 0))
    rank = jnp.sum(jnp.where(earlier, 1.0, 0.0), axis=1, keepdims=True).astype(jnp.int32)
    frame = down[:, :1].astype(jnp.int32)
    rows = block_rows(slots)
    inside = (rank >= base) & (rank < base + slots)
    fine_at = jnp.where(inside, frame * rows + rank - base, -1)
    coarse_at = jnp.where(inside, frame * rows + slots + rank - base, -1)
    place = iota((points, devices * rows), 1)
    chosen = [jnp.where(place == at, 1.0, 0.0).astype(BF16) for at in (fine_at, coarse_at)]
    return jnp.concatenate(chosen, axis=0)


def prepare_kernel(
    slots,
    row_hbm,
    column_hbm,
    query_hbm,
    window_hbm,
    match_hbm,
    map_ref,
    packed_ref,
    rounds_ref,
    chosen_ref,
    fine_ref,
    coarse_ref,
    spread_ref,
    embedding_ref,
    row_ref,
    column_ref,
    query_ref,
    window_ref,
    match_ref,
    corners_ref,
    corner_at,
    cells,
    fine_map,
    coarse_map,
    map_sems,
    sems,
):
    chunks, depth, breadth, channels = cells.shape
    height = chunks * depth
    half = breadth // 2
    copies = [
        pltpu.make_async_copy(source, target, sems.at[index])
        for index, (source, target) in enumerate(
            (
                (row_hbm, row_ref),
                (column_hbm, column_ref),
                (query_hbm, query_ref),
                (window_hbm, window_ref),
                (match_hbm, match_ref),
            )
        )
    ]
    for copy in copies:
        copy.start()
    for chunk in range(chunks):
        map_copy(map_ref, cells, map_sems, chunk).start()
    me = lax.axis_index("frame")
    points = query_ref.shape[1]
    rows = block_rows(slots)
    devices = packed_ref.shape[0] // rows
    place = iota((2 * SPAN, match_ref.shape[0]), 0)
    level, k, m = place >> 6, (place & (SPAN - 1)) >> 3, place & 7
    at = jnp.where((k < PATCH) & (m < PATCH), (level * PATCH + k) * PATCH + m, -1)
    pick = jnp.where(iota(place.shape, 1) == at, 1.0, 0.0).astype(BF16)
    lane = iota((half, 2 * breadth), 1)
    pool = jnp.where(jnp.where(lane < breadth, lane, lane - breadth) >> 1 == iota(lane.shape, 0), 0.25, 0.0)
    pool = pool.astype(BF16)
    coarse_map[pl.ds(height // 2 * half, 8), :] = jnp.zeros((8, channels), F32)
    features = embedding_ref.shape[1]
    feature = iota((1, features), 1)
    of_sine = feature < features // 2
    step = jnp.where(of_sine, feature, feature - features // 2).astype(F32)
    frequency = jnp.exp(-math.log(10000.0) * step / (features // 2))
    for copy in copies[:4]:
        copy.wait()
    row, column, query = row_ref[...], column_ref[...], query_ref[...]
    corners_ref[0:1, :] = row * breadth + column - (3 * breadth + 3)
    corners_ref[1:2, :] = (row >> 1) * half + (column >> 1) - (3 * half + 3)
    corner_copy = pltpu.make_async_copy(corners_ref, corner_at, sems.at[5])
    corner_copy.start()
    is_fine, wanted = slot_cells(slots, 0, query, row, column, breadth)
    chosen_ref[...] = choose(query, devices, slots, 0)
    there = jnp.where(iota((devices, points), 0) == query, 1.0, 0.0)
    load = jnp.max(jnp.sum(there, axis=1, keepdims=True)).astype(jnp.int32)
    rounds_ref[0] = (load + slots - 1) // slots
    copies[4].wait()
    spread_ref[...] = matmul(pick, match_ref[...]).astype(BF16)
    angle = (window_ref[0, 0] + me).astype(F32) * frequency
    embedding_ref[...] = jnp.where(of_sine, jnp.sin(angle), jnp.cos(angle))

    def convert(pair, both, total):
        product = matmul(jnp.concatenate([pool, slot_weights(is_fine, wanted, pair, breadth)], axis=0), both)
        fine_map[pl.ds(pl.multiple_of(pair * 2 * breadth, 2 * breadth), 2 * breadth), :] = both.astype(F32)
        coarse_map[pl.ds(pl.multiple_of(pair * half, half), half), :] = product[:half].astype(BF16).astype(F32)
        return total + product[half:]

    total = each_pair(map_ref, cells, map_sems, convert, jnp.zeros((wanted.shape[0], channels), F32))
    send_block(total, rows, packed_ref)
    blank = jnp.zeros((8, channels), F32)
    corner_copy.wait()

    def gather(point, carry):
        for level, (ref, wide, out) in enumerate(((fine_map, breadth, fine_ref), (coarse_map, half, coarse_ref))):
            window = ref.at[pl.ds(corner_at[level, point], 6 * wide + 8), :]
            target = out.at[pl.ds(pl.multiple_of(point * SPAN, SPAN), SPAN), :]
            lines = [window[k * wide : k * wide + 8, :] for k in range(PATCH)] + [blank]
            for t in range(4):
                target[t * TILE : (t + 1) * TILE, :] = jnp.concatenate(lines[2 * t : 2 * t + 2], axis=0).astype(BF16)
        return carry

    lax.fori_loop(0, points, gather, 0, unroll=8)


def attention(queries, keyset, values, bias):
    rows, features = queries.shape
    per_head = features // HEADS
    head_of = iota((1, features), 1) // per_head
    spread = jnp.concatenate([jnp.where(head_of == head, queries, 0) for head in range(HEADS)], axis=0)
    scores = matmul_nt(spread, keyset)
    parts = []
    for head in range(HEADS):
        part = scores[head * rows : (head + 1) * rows] + bias
        part = part - jnp.max(part, axis=-1, keepdims=True)
        part = jnp.exp2(part * (math.log2(math.e) / math.sqrt(per_head)))
        parts.append((part * (1.0 / jnp.sum(part, axis=-1, keepdims=True))).astype(BF16))
    apart = jnp.concatenate([jnp.where(head_of == head, values, 0) for head in range(HEADS)], axis=0)
    return matmul(jnp.concatenate(parts, axis=1), apart).astype(BF16)


def gelu(value):
    inner = math.sqrt(2.0 / math.pi)
    lifted = value * (inner + (inner * 0.044715) * (value * value))
    half = 0.5 * value
    return half + half * jnp.tanh(lifted)


def finish(stream, attended, gain, output_weight, expand_weight, reduce_weight):
    stream = stream + matmul(attended, output_weight())
    hidden = normalize(stream, gain).astype(BF16)
    widened = gelu(matmul(hidden, expand_weight())).astype(BF16)
    return stream + matmul(widened, reduce_weight())


def frame_kernel(
    extra_ref,
    received_ref,
    chosen_ref,
    fine_ref,
    coarse_ref,
    spread_ref,
    embedding_ref,
    visible_ref,
    gains_ref,
    *refs,
):
    sources, out_ref, staged, held, sems = refs[:4], refs[4], refs[5], refs[6:10], refs[10]
    copies = [
        pltpu.make_async_copy(source.at[0], target, sems.at[index])
        for index, (source, target) in enumerate(zip(sources, held))
    ]
    for copy in copies:
        copy.start()

    def weight(index):
        def ready():
            copies[index].wait()
            return held[index][...]

        return ready

    me = lax.axis_index("frame")
    points = visible_ref.shape[1]
    channels = received_ref.shape[1]
    features = spread_ref.shape[1]
    devices, pad_rows, _ = out_ref.shape
    anchors = matmul(chosen_ref[...], received_ref[...])
    if extra_ref is not None:
        anchors = anchors + extra_ref[...].astype(F32)
    line, lane = iota((8, LANES), 0), iota((8, LANES), 1)
    none = jnp.zeros((8, channels), F32)
    rows = []
    for start in range(0, points, 8):
        fine, coarse = anchors[start : start + 8], anchors[points + start : points + start + 8]
        both = jnp.concatenate(
            [jnp.concatenate([fine, none], axis=1), jnp.concatenate([none, coarse], axis=1)], axis=0
        ).astype(BF16)
        span = slice(start * SPAN, (start + 8) * SPAN)
        scores = matmul_nt(both, jnp.concatenate([fine_ref[span, :], coarse_ref[span, :]], axis=1))
        sides = []
        for level in range(2):
            own = scores[level * 8 : level * 8 + 8]
            kept = own[:, :LANES]
            for index in range(1, 4):
                kept = jnp.where(line // 2 == index, own[:, index * LANES : (index + 1) * LANES], kept)
            sides.append(jnp.where(line % 2 == level, kept, pltpu.roll(kept, SPAN, 1)))
        rows.append(jnp.where(lane < SPAN, sides[0], sides[1]))
    matches = (jnp.concatenate(rows, axis=0) * (1.0 / math.sqrt(channels))).astype(BF16)
    tokens = (matmul(matches, spread_ref[...]) + embedding_ref[...]).astype(BF16)

    stream = tokens.astype(F32)
    hidden = normalize(stream, gains_ref[0, 0:1, :]).astype(BF16)
    projected = matmul(hidden, weight(0)()).astype(BF16)
    allowed = visible_ref[pl.ds(me, 1), :] == 1
    permitted = allowed | (iota((points, points), 0) == iota((points, points), 1))
    attended = attention(
        projected[:, :features],
        projected[:, features : 2 * features],
        projected[:, 2 * features :],
        jnp.where(permitted, 0.0, -1e30),
    )
    crossed = finish(stream, attended, gains_ref[0, 1:2, :], weight(1), weight(2), weight(3))
    chunks = features // LANES
    for i in range(points // devices):
        for c in range(chunks):
            staged[pl.ds(i * chunks + c, devices, stride=pad_rows), :] = crossed[
                i * devices : (i + 1) * devices, c * LANES : (c + 1) * LANES
            ]
    out_ref[...] = staged[...].astype(BF16).reshape(out_ref.shape)


def track_kernel(
    per_device,
    received_ref,
    visible_ref,
    gains_ref,
    joint_ref,
    output_ref,
    expand_ref,
    reduce_ref,
    out_ref,
    staged,
):
    me = lax.axis_index("frame")
    length, pad_rows, _ = received_ref.shape
    features = output_ref.shape[1]
    chunks = features // LANES
    points = visible_ref.shape[1]
    devices = out_ref.shape[0]
    half_way = length // 2
    staged[...] = received_ref[...].reshape(length * pad_rows, LANES).astype(F32)
    stream = jnp.concatenate(
        [
            jnp.concatenate(
                [staged[pl.ds(i * chunks + c, length, stride=pad_rows), :] for c in range(chunks)], axis=1
            )
            for i in range(per_device)
        ],
        axis=0,
    )
    total = per_device * length
    hidden = normalize(stream, gains_ref[1, 0:1, :]).astype(BF16)
    projected = matmul(hidden, joint_ref[1]).astype(BF16)

    def later(array):
        return jnp.concatenate(
            [array[i * length + half_way : (i + 1) * length] for i in range(per_device)], axis=0
        )

    rest = length - half_way
    lane = iota((points, total), 1)
    pick = jnp.where(iota((points, total), 0) == lane // length * devices + me, 1.0, 0.0).astype(BF16)
    seen = matmul(jnp.where(visible_ref[...] == 1, 1.0, 0.0).astype(BF16), pick)
    seen = jnp.where(iota((length, total), 1) % length == iota((length, total), 0), seen, 0.0)
    allowed = jnp.sum(seen, axis=0, keepdims=True) > 0.5
    query_at = iota((per_device * rest, total), 0)
    key_at = iota((per_device * rest, total), 1)
    same_point = query_at // rest == key_at // length
    same_frame = query_at % rest + half_way == key_at % length
    permitted = same_point & (allowed | same_frame)
    attended = attention(
        later(projected[:, :features]),
        projected[:, features : 2 * features],
        projected[:, 2 * features :],
        jnp.where(permitted, 0.0, -1e30),
    )
    tracked = finish(
        later(stream),
        attended,
        gains_ref[1, 1:2, :],
        lambda: output_ref[1],
        lambda: expand_ref[1],
        lambda: reduce_ref[1],
    )
    for i in range(per_device):
        for c in range(chunks):
            piece = tracked[i * rest : (i + 1) * rest, c * LANES : (c + 1) * LANES]
            at = i * chunks + c
            staged[pl.ds(at, rest, stride=pad_rows), :] = piece
            staged[pl.ds(rest * pad_rows + at, half_way, stride=pad_rows), :] = jnp.broadcast_to(
                piece[rest - 1 :], (half_way, LANES)
            )
    out_ref[...] = staged[...].astype(BF16).reshape(out_ref.shape)


def layout_kernel(received_ref, out_ref, staged):
    devices, pad_rows, _ = received_ref.shape
    _, points, features = out_ref.shape
    chunks = features // LANES
    staged[...] = received_ref[...].reshape(devices * pad_rows, LANES).astype(F32)
    for i in range(points // devices):
        for c in range(chunks):
            out_ref[0, i * devices : (i + 1) * devices, c * LANES : (c + 1) * LANES] = staged[
                pl.ds(i * chunks + c, devices, stride=pad_rows), :
            ].astype(BF16)


def exchange(block):
    return lax.all_to_all(block, "frame", split_axis=0, concat_axis=0, tiled=True)


def step(
    further,
    feature_map,
    pixel_row,
    pixel_column,
    query_frame,
    visible,
    window_start,
    match_weight,
    layer_gains,
    *weights,
):
    _, height, breadth, channels = feature_map.shape
    points = query_frame.shape[0]
    features = match_weight.shape[1]
    devices = lax.axis_size("frame")
    per_device = points // devices
    slots = 3 * per_device
    rows = block_rows(slots)
    pad_rows = TILE * -(-per_device * (features // LANES) // TILE)
    query_row = query_frame.reshape(1, points)
    vmem = pl.BlockSpec(memory_space=VMEM)
    smem = pl.BlockSpec(memory_space=SMEM)
    here = pl.BlockSpec(memory_space=pltpu.MemorySpace.HBM)
    chunks = 8
    map_scratch = pltpu.VMEM((chunks, height // chunks, breadth, channels), BF16)
    map_sems = pltpu.SemaphoreType.DMA((chunks,))
    block = jax.ShapeDtypeStruct((devices * rows, channels), BF16)

    line = pltpu.VMEM((1, points), jnp.int32)
    packed, rounds, *prepared = pl.pallas_call(
        lambda *refs: prepare_kernel(slots, *refs),
        out_shape=[
            block,
            jax.ShapeDtypeStruct((1,), jnp.int32),
            jax.ShapeDtypeStruct((2 * points, devices * rows), BF16),
            jax.ShapeDtypeStruct((points * SPAN, channels), BF16),
            jax.ShapeDtypeStruct((points * SPAN, channels), BF16),
            jax.ShapeDtypeStruct((2 * SPAN, features), BF16),
            jax.ShapeDtypeStruct((1, features), F32),
        ],
        in_specs=[here] * 6,
        out_specs=[vmem, smem] + [vmem] * 5,
        scratch_shapes=[
            line,
            line,
            line,
            pltpu.SMEM((1, 1), jnp.int32),
            pltpu.VMEM(match_weight.shape, BF16),
            pltpu.VMEM((2, points), jnp.int32),
            pltpu.SMEM((2, points), jnp.int32),
            map_scratch,
            pltpu.VMEM((height * breadth, channels), F32),
            pltpu.VMEM((height * breadth // 4 + 8, channels), F32),
            map_sems,
            pltpu.SemaphoreType.DMA((6,)),
        ],
        compiler_params=pltpu.CompilerParams(vmem_limit_bytes=(16 + points // 16) * MIB),
        name="prepare",
    )(pixel_row, pixel_column, query_row, window_start.reshape(1, 1), match_weight, feature_map)
    rounds = rounds.reshape(())
    received = exchange(packed)
    extra = ()
    if further:

        def next_round(state):
            which, extra = state
            again = pl.pallas_call(
                lambda *refs: pack_again_kernel(slots, *refs),
                out_shape=block,
                in_specs=[smem, vmem, vmem, vmem, here],
                out_specs=vmem,
                scratch_shapes=[map_scratch, map_sems],
                compiler_params=pltpu.CompilerParams(vmem_limit_bytes=8 * MIB),
                name="pack_again",
            )(which.reshape(1), query_row, pixel_row, pixel_column, feature_map)
            extra = pl.pallas_call(
                lambda *refs: unpack_again_kernel(slots, devices, *refs),
                out_shape=jax.ShapeDtypeStruct(extra.shape, BF16),
                in_specs=[smem, vmem, vmem, vmem],
                out_specs=vmem,
                compiler_params=pltpu.CompilerParams(vmem_limit_bytes=(4 + points // 16) * MIB),
                name="unpack_again",
            )(which.reshape(1), query_row, exchange(again), extra)
            return which + 1, extra

        received, rounds = lax.optimization_barrier((received, lax.pmax(rounds, "groups")))
        start = (jnp.int32(1), jnp.zeros((2 * points, channels), BF16))
        extra = lax.while_loop(lambda state: state[0] < rounds, next_round, start)[1:]
    crossed = pl.pallas_call(
        frame_kernel if further else lambda *refs: frame_kernel(None, *refs),
        out_shape=jax.ShapeDtypeStruct((devices, pad_rows, LANES), BF16),
        in_specs=[vmem] * (8 + len(extra)) + [here] * 4,
        out_specs=vmem,
        scratch_shapes=[
            pltpu.VMEM((devices * pad_rows, LANES), F32),
            *(pltpu.VMEM(array.shape[1:], BF16) for array in weights),
            pltpu.SemaphoreType.DMA((4,)),
        ],
        compiler_params=pltpu.CompilerParams(vmem_limit_bytes=(12 + points // 16) * MIB),
        name="frame_block",
    )(*extra, received, *prepared, visible, layer_gains, *weights)
    by_track = exchange(crossed)
    tracked = pl.pallas_call(
        lambda *refs: track_kernel(per_device, *refs),
        out_shape=jax.ShapeDtypeStruct((devices, pad_rows, LANES), BF16),
        in_specs=[vmem] * 7,
        out_specs=vmem,
        scratch_shapes=[pltpu.VMEM((devices * pad_rows, LANES), F32)],
        compiler_params=pltpu.CompilerParams(vmem_limit_bytes=(4 + points // 16) * MIB),
        name="track_block",
    )(by_track, visible, layer_gains, *weights)
    arrived = exchange(tracked)
    handed = pl.pallas_call(
        layout_kernel,
        out_shape=jax.ShapeDtypeStruct((1, points, features), BF16),
        in_specs=[vmem],
        out_specs=vmem,
        scratch_shapes=[pltpu.VMEM((devices * pad_rows, LANES), F32)],
        compiler_params=pltpu.CompilerParams(vmem_limit_bytes=4 * MIB),
        name="layout",
    )(arrived)
    return rounds, handed


def shards(*arrays):
    rounds, handed = step(False, *arrays)

    def again(state):
        rounds, _ = state
        return jnp.int32(1), step(True, *lax.optimization_barrier((rounds,) + arrays)[1:])[1]

    return lax.while_loop(lambda state: state[0] > 1, again, (lax.pmax(rounds, "groups"), handed))[1]


def solution(mesh):
    placed = (
        P("frame", "groups", None, None),
        P("frame", "groups"),
        P("frame", "groups"),
        P("groups"),
        P(None, "groups"),
        P("groups"),
        P(),
        P(),
        P(),
        P(),
        P(),
        P(),
    )
    return jax.shard_map(
        shards, mesh=mesh, in_specs=placed, out_specs=P("frame", "groups", None), check_vma=False
    )
```

```python
import math

import jax
import jax.numpy as jnp
from jax import lax
from jax.experimental import pallas as pl
from jax.experimental.pallas import tpu as pltpu
from jax.sharding import PartitionSpec as P

HEADS = 8
PATCH = 7
EPSILON = 1e-05
LANES = 128
TILE = 16
SPAN = 64
SHARE = 3
MIB = 1 << 20
F32 = jnp.float32
BF16 = jnp.bfloat16
VMEM = pltpu.MemorySpace.VMEM
SMEM = pltpu.MemorySpace.SMEM


def normalize(values, weights):
    average = jnp.mean(values, axis=-1, keepdims=True)
    centred = values - average
    variance = jnp.mean(centred * centred, axis=-1, keepdims=True)
    return centred * lax.rsqrt(variance + EPSILON) * weights


def iota(shape, axis):
    return lax.broadcasted_iota(jnp.int32, shape, axis)


def matmul(left, right):
    return jnp.dot(left, right, preferred_element_type=F32)


def matmul_nt(left, right):
    return lax.dot_general(left, right, (((1,), (1,)), ((), ())), preferred_element_type=F32)


def slot_cells(per_device, base, query, row, column, breadth):
    me = lax.axis_index("frame")
    points = query.shape[1]
    slots = SHARE * per_device
    mine = query == me
    before = jnp.where(iota((points, points), 0) < iota((points, points), 1), 1.0, 0.0).astype(BF16)
    rank = matmul(jnp.broadcast_to(jnp.where(mine, 1.0, 0.0), (8, points)).astype(BF16), before)[:1]
    slot = jnp.where(mine, rank.astype(jnp.int32) - base, -1)
    rows = TILE * -(-2 * slots // TILE)
    line = iota((rows, 1), 0)
    is_fine = line < slots
    held = jnp.where(is_fine, line, line - slots) == jnp.where(slot < slots, slot, -1)

    def gathered(values):
        return jnp.sum(jnp.where(held, values + 1, 0).astype(F32), axis=1, keepdims=True).astype(jnp.int32) - 1

    fine_at = gathered(row * breadth + column)
    coarse_at = gathered((row >> 1) * (breadth // 2) + (column >> 1))
    return is_fine, jnp.where(is_fine, fine_at, coarse_at)


def slot_weights(is_fine, wanted, pair, breadth):
    lane = iota((1, 2 * breadth), 1)
    column = jnp.where(lane < breadth, lane, lane - breadth)
    places = jnp.where(is_fine, lane, column >> 1)
    start = jnp.where(is_fine, pair * (2 * breadth), pair * (breadth // 2))
    return jnp.where(places == wanted - start, jnp.where(is_fine, 1.0, 0.25), 0.0).astype(BF16)


def send_block(total, out_ref):
    per_device = out_ref.shape[1]
    starts = [(level * SHARE + part) * per_device for part in range(SHARE) for level in range(2)]
    pieces = [total[start : start + per_device] for start in starts]
    block = jnp.concatenate(pieces, axis=1).astype(BF16)
    out_ref[...] = jnp.broadcast_to(block[None], out_ref.shape)


def map_copy(map_ref, cells, sems, chunk):
    depth = cells.shape[1]
    return pltpu.make_async_copy(map_ref.at[0, pl.ds(chunk * depth, depth)], cells.at[chunk], sems.at[chunk])


def each_pair(map_ref, cells, sems, body, carry):
    chunks, depth, breadth, channels = cells.shape

    def walk(chunk, carry):
        map_copy(map_ref, cells, sems, chunk).wait()
        for inner in range(depth // 2):
            both = cells[chunk, 2 * inner : 2 * inner + 2].reshape(2 * breadth, channels)
            carry = body(chunk * (depth // 2) + inner, both, carry)
        return carry

    return lax.fori_loop(0, chunks, walk, carry)


def pack_again_kernel(round_ref, query_ref, row_ref, column_ref, map_ref, out_ref, cells, sems):
    chunks, _, breadth, channels = cells.shape
    per_device = out_ref.shape[1]
    for chunk in range(chunks):
        map_copy(map_ref, cells, sems, chunk).start()
    base = round_ref[0] * SHARE * per_device
    is_fine, wanted = slot_cells(per_device, base, query_ref[...], row_ref[...], column_ref[...], breadth)

    def body(pair, both, total):
        return total + matmul(slot_weights(is_fine, wanted, pair, breadth), both)

    total = each_pair(map_ref, cells, sems, body, jnp.zeros((wanted.shape[0], channels), F32))
    send_block(total, out_ref)


def choose(query_row, devices, per_device, base):
    points = query_row.shape[1]
    across = jnp.broadcast_to(query_row.astype(F32), (points, points))
    down = across.T
    earlier = (across == down) & (iota((points, points), 1) < iota((points, points), 0))
    rank = jnp.sum(jnp.where(earlier, 1.0, 0.0), axis=1, keepdims=True).astype(jnp.int32) - base
    frame = down[:, :1].astype(jnp.int32)
    inside = (rank >= 0) & (rank < SHARE * per_device)
    at = (rank // per_device * devices + frame) * per_device + rank % per_device
    place = iota((points, SHARE * devices * per_device), 1)
    return jnp.where(place == jnp.where(inside, at, -1), 1.0, 0.0).astype(BF16)


def take(chosen, received_ref):
    devices, per_device, width = received_ref.shape
    flat = received_ref[...].reshape(devices * per_device, width)
    share = width // SHARE
    return matmul(chosen, jnp.concatenate([flat[:, g * share : (g + 1) * share] for g in range(SHARE)], axis=0))


def unpack_again_kernel(round_ref, query_ref, received_ref, before_ref, out_ref):
    devices, per_device, _ = received_ref.shape
    chosen = choose(query_ref[...], devices, per_device, round_ref[0] * SHARE * per_device)
    out_ref[...] = before_ref[...] + take(chosen, received_ref).astype(BF16)


def prepare_kernel(
    row_hbm,
    column_hbm,
    query_hbm,
    window_hbm,
    match_hbm,
    map_ref,
    packed_ref,
    rounds_ref,
    chosen_ref,
    fine_ref,
    coarse_ref,
    spread_ref,
    embedding_ref,
    row_ref,
    column_ref,
    query_ref,
    window_ref,
    match_ref,
    corners_ref,
    corner_at,
    cells,
    fine_map,
    coarse_map,
    map_sems,
    sems,
):
    chunks, depth, breadth, channels = cells.shape
    height = chunks * depth
    half = breadth // 2
    copies = [
        pltpu.make_async_copy(source, target, sems.at[index])
        for index, (source, target) in enumerate(
            (
                (row_hbm, row_ref),
                (column_hbm, column_ref),
                (query_hbm, query_ref),
                (window_hbm, window_ref),
                (match_hbm, match_ref),
            )
        )
    ]
    for copy in copies:
        copy.start()
    for chunk in range(chunks):
        map_copy(map_ref, cells, map_sems, chunk).start()
    me = lax.axis_index("frame")
    points = query_ref.shape[1]
    devices, per_device, _ = packed_ref.shape
    slots = SHARE * per_device
    place = iota((2 * SPAN, match_ref.shape[0]), 0)
    level, k, m = place >> 6, (place & (SPAN - 1)) >> 3, place & 7
    at = jnp.where((k < PATCH) & (m < PATCH), (level * PATCH + k) * PATCH + m, -1)
    pick = jnp.where(iota(place.shape, 1) == at, 1.0, 0.0).astype(BF16)
    lane = iota((half, 2 * breadth), 1)
    pool = jnp.where(jnp.where(lane < breadth, lane, lane - breadth) >> 1 == iota(lane.shape, 0), 0.25, 0.0)
    pool = pool.astype(BF16)
    coarse_map[pl.ds(height // 2 * half, 8), :] = jnp.zeros((8, channels), F32)
    features = embedding_ref.shape[1]
    feature = iota((1, features), 1)
    of_sine = feature < features // 2
    step = jnp.where(of_sine, feature, feature - features // 2).astype(F32)
    frequency = jnp.exp(-math.log(10000.0) * step / (features // 2))
    for copy in copies[:4]:
        copy.wait()
    row, column, query = row_ref[...], column_ref[...], query_ref[...]
    corners_ref[0:1, :] = row * breadth + column - (3 * breadth + 3)
    corners_ref[1:2, :] = (row >> 1) * half + (column >> 1) - (3 * half + 3)
    corner_copy = pltpu.make_async_copy(corners_ref, corner_at, sems.at[5])
    corner_copy.start()
    is_fine, wanted = slot_cells(per_device, 0, query, row, column, breadth)
    chosen_ref[...] = choose(query, devices, per_device, 0)
    there = jnp.where(iota((devices, points), 0) == query, 1.0, 0.0)
    load = jnp.max(jnp.sum(there, axis=1, keepdims=True)).astype(jnp.int32)
    rounds_ref[0] = (load + slots - 1) // slots
    copies[4].wait()
    spread_ref[...] = matmul(pick, match_ref[...]).astype(BF16)
    angle = (window_ref[0, 0] + me).astype(F32) * frequency
    embedding_ref[...] = jnp.where(of_sine, jnp.sin(angle), jnp.cos(angle))

    def convert(pair, both, total):
        product = matmul(jnp.concatenate([pool, slot_weights(is_fine, wanted, pair, breadth)], axis=0), both)
        fine_map[pl.ds(pl.multiple_of(pair * 2 * breadth, 2 * breadth), 2 * breadth), :] = both.astype(F32)
        coarse_map[pl.ds(pl.multiple_of(pair * half, half), half), :] = product[:half].astype(BF16).astype(F32)
        return total + product[half:]

    total = each_pair(map_ref, cells, map_sems, convert, jnp.zeros((wanted.shape[0], channels), F32))
    send_block(total, packed_ref)
    blank = jnp.zeros((8, channels), F32)
    corner_copy.wait()

    def gather(point, carry):
        for level, (ref, wide, out) in enumerate(((fine_map, breadth, fine_ref), (coarse_map, half, coarse_ref))):
            window = ref.at[pl.ds(corner_at[level, point], 6 * wide + 8), :]
            target = out.at[pl.ds(pl.multiple_of(point * SPAN, SPAN), SPAN), :]
            lines = [window[k * wide : k * wide + 8, :] for k in range(PATCH)] + [blank]
            for t in range(4):
                target[t * TILE : (t + 1) * TILE, :] = jnp.concatenate(lines[2 * t : 2 * t + 2], axis=0).astype(BF16)
        return carry

    lax.fori_loop(0, points, gather, 0, unroll=8)


def attention(queries, keyset, values, bias):
    rows, features = queries.shape
    per_head = features // HEADS
    head_of = iota((1, features), 1) // per_head
    spread = jnp.concatenate([jnp.where(head_of == head, queries, 0) for head in range(HEADS)], axis=0)
    scores = matmul_nt(spread, keyset)
    parts = []
    for head in range(HEADS):
        part = scores[head * rows : (head + 1) * rows] + bias
        part = part - jnp.max(part, axis=-1, keepdims=True)
        part = jnp.exp2(part * (math.log2(math.e) / math.sqrt(per_head)))
        parts.append((part * (1.0 / jnp.sum(part, axis=-1, keepdims=True))).astype(BF16))
    apart = jnp.concatenate([jnp.where(head_of == head, values, 0) for head in range(HEADS)], axis=0)
    return matmul(jnp.concatenate(parts, axis=1), apart).astype(BF16)


def gelu(value):
    inner = math.sqrt(2.0 / math.pi)
    lifted = value * (inner + (inner * 0.044715) * (value * value))
    half = 0.5 * value
    return half + half * jnp.tanh(lifted)


def finish(stream, attended, gain, output_weight, expand_weight, reduce_weight):
    stream = stream + matmul(attended, output_weight())
    hidden = normalize(stream, gain).astype(BF16)
    widened = gelu(matmul(hidden, expand_weight())).astype(BF16)
    return stream + matmul(widened, reduce_weight())


def frame_kernel(
    extra_ref,
    received_ref,
    chosen_ref,
    fine_ref,
    coarse_ref,
    spread_ref,
    embedding_ref,
    visible_ref,
    gains_ref,
    *refs,
):
    sources, out_ref, held, sems = refs[:4], refs[4], refs[5:9], refs[9]
    copies = [
        pltpu.make_async_copy(source.at[0], target, sems.at[index])
        for index, (source, target) in enumerate(zip(sources, held))
    ]
    for copy in copies:
        copy.start()

    def weight(index):
        def ready():
            copies[index].wait()
            return held[index][...]

        return ready

    me = lax.axis_index("frame")
    points = visible_ref.shape[1]
    channels = fine_ref.shape[1]
    features = spread_ref.shape[1]
    anchors = take(chosen_ref[...], received_ref)
    if extra_ref is not None:
        anchors = anchors + extra_ref[...].astype(F32)
    line, lane = iota((8, LANES), 0), iota((8, LANES), 1)
    none = jnp.zeros((8, channels), F32)
    rows = []
    for start in range(0, points, 8):
        fine, coarse = anchors[start : start + 8, :channels], anchors[start : start + 8, channels:]
        both = jnp.concatenate(
            [jnp.concatenate([fine, none], axis=1), jnp.concatenate([none, coarse], axis=1)], axis=0
        ).astype(BF16)
        span = slice(start * SPAN, (start + 8) * SPAN)
        scores = matmul_nt(both, jnp.concatenate([fine_ref[span, :], coarse_ref[span, :]], axis=1))
        sides = []
        for level in range(2):
            own = scores[level * 8 : level * 8 + 8]
            kept = own[:, :LANES]
            for index in range(1, 4):
                kept = jnp.where(line // 2 == index, own[:, index * LANES : (index + 1) * LANES], kept)
            sides.append(jnp.where(line % 2 == level, kept, pltpu.roll(kept, SPAN, 1)))
        rows.append(jnp.where(lane < SPAN, sides[0], sides[1]))
    matches = (jnp.concatenate(rows, axis=0) * (1.0 / math.sqrt(channels))).astype(BF16)
    tokens = (matmul(matches, spread_ref[...]) + embedding_ref[...]).astype(BF16)

    stream = tokens.astype(F32)
    hidden = normalize(stream, gains_ref[0, 0:1, :]).astype(BF16)
    projected = matmul(hidden, weight(0)()).astype(BF16)
    allowed = visible_ref[pl.ds(me, 1), :] == 1
    permitted = allowed | (iota((points, points), 0) == iota((points, points), 1))
    attended = attention(
        projected[:, :features],
        projected[:, features : 2 * features],
        projected[:, 2 * features :],
        jnp.where(permitted, 0.0, -1e30),
    )
    crossed = finish(stream, attended, gains_ref[0, 1:2, :], weight(1), weight(2), weight(3))
    out_ref[...] = crossed.astype(BF16).reshape(out_ref.shape)


def track_kernel(received_ref, visible_ref, gains_ref, joint_ref, output_ref, expand_ref, reduce_ref, out_ref):
    me = lax.axis_index("frame")
    length, per_device, features = received_ref.shape
    points = visible_ref.shape[1]
    half_way = length // 2
    rest = length - half_way
    total = length * per_device
    skipped = half_way * per_device
    stream = received_ref[...].astype(F32).reshape(total, features)
    hidden = normalize(stream, gains_ref[1, 0:1, :]).astype(BF16)
    projected = matmul(hidden, joint_ref[1]).astype(BF16)
    pick = iota((points, total), 0) == me * per_device + iota((points, total), 1) % per_device
    seen = matmul(jnp.where(visible_ref[...] == 1, 1.0, 0.0).astype(BF16), jnp.where(pick, 1.0, 0.0).astype(BF16))
    seen = jnp.where(iota((length, total), 1) // per_device == iota((length, total), 0), seen, 0.0)
    allowed = jnp.sum(seen, axis=0, keepdims=True) > 0.5
    query_at = iota((rest * per_device, total), 0) + skipped
    key_at = iota((rest * per_device, total), 1)
    same_point = query_at % per_device == key_at % per_device
    permitted = same_point & (allowed | (query_at == key_at))
    attended = attention(
        projected[skipped:, :features],
        projected[:, features : 2 * features],
        projected[:, 2 * features :],
        jnp.where(permitted, 0.0, -1e30),
    )
    tracked = finish(
        stream[skipped:],
        attended,
        gains_ref[1, 1:2, :],
        lambda: output_ref[1],
        lambda: expand_ref[1],
        lambda: reduce_ref[1],
    )
    tracked = tracked.astype(BF16).reshape(rest, per_device, features)
    out_ref[:rest] = tracked
    out_ref[rest:] = jnp.broadcast_to(tracked[rest - 1 :], (half_way, per_device, features))


def layout_kernel(received_ref, out_ref):
    out_ref[...] = received_ref[...].astype(F32).reshape(out_ref.shape).astype(BF16)


def exchange(block):
    return lax.all_to_all(block, "frame", split_axis=0, concat_axis=0, tiled=True)


def step(
    further,
    feature_map,
    pixel_row,
    pixel_column,
    query_frame,
    visible,
    window_start,
    match_weight,
    layer_gains,
    *weights,
):
    _, height, breadth, channels = feature_map.shape
    points = query_frame.shape[0]
    features = match_weight.shape[1]
    devices = lax.axis_size("frame")
    per_device = points // devices
    query_row = query_frame.reshape(1, points)
    vmem = pl.BlockSpec(memory_space=VMEM)
    smem = pl.BlockSpec(memory_space=SMEM)
    here = pl.BlockSpec(memory_space=pltpu.MemorySpace.HBM)
    chunks = 8
    map_scratch = pltpu.VMEM((chunks, height // chunks, breadth, channels), BF16)
    map_sems = pltpu.SemaphoreType.DMA((chunks,))
    block = jax.ShapeDtypeStruct((devices, per_device, SHARE * 2 * channels), BF16)
    shares = jax.ShapeDtypeStruct((devices, per_device, features), BF16)

    line = pltpu.VMEM((1, points), jnp.int32)
    packed, rounds, *prepared = pl.pallas_call(
        prepare_kernel,
        out_shape=[
            block,
            jax.ShapeDtypeStruct((1,), jnp.int32),
            jax.ShapeDtypeStruct((points, SHARE * devices * per_device), BF16),
            jax.ShapeDtypeStruct((points * SPAN, channels), BF16),
            jax.ShapeDtypeStruct((points * SPAN, channels), BF16),
            jax.ShapeDtypeStruct((2 * SPAN, features), BF16),
            jax.ShapeDtypeStruct((1, features), F32),
        ],
        in_specs=[here] * 6,
        out_specs=[vmem, smem] + [vmem] * 5,
        scratch_shapes=[
            line,
            line,
            line,
            pltpu.SMEM((1, 1), jnp.int32),
            pltpu.VMEM(match_weight.shape, BF16),
            pltpu.VMEM((2, points), jnp.int32),
            pltpu.SMEM((2, points), jnp.int32),
            map_scratch,
            pltpu.VMEM((height * breadth, channels), F32),
            pltpu.VMEM((height * breadth // 4 + 8, channels), F32),
            map_sems,
            pltpu.SemaphoreType.DMA((6,)),
        ],
        compiler_params=pltpu.CompilerParams(vmem_limit_bytes=(16 + points // 16) * MIB),
        name="prepare",
    )(pixel_row, pixel_column, query_row, window_start.reshape(1, 1), match_weight, feature_map)
    rounds = rounds.reshape(())
    received = exchange(packed)
    extra = ()
    if further:

        def next_round(state):
            which, extra = state
            again = pl.pallas_call(
                pack_again_kernel,
                out_shape=block,
                in_specs=[smem, vmem, vmem, vmem, here],
                out_specs=vmem,
                scratch_shapes=[map_scratch, map_sems],
                compiler_params=pltpu.CompilerParams(vmem_limit_bytes=8 * MIB),
                name="pack_again",
            )(which.reshape(1), query_row, pixel_row, pixel_column, feature_map)
            extra = pl.pallas_call(
                unpack_again_kernel,
                out_shape=jax.ShapeDtypeStruct(extra.shape, BF16),
                in_specs=[smem, vmem, vmem, vmem],
                out_specs=vmem,
                compiler_params=pltpu.CompilerParams(vmem_limit_bytes=(4 + points // 16) * MIB),
                name="unpack_again",
            )(which.reshape(1), query_row, exchange(again), extra)
            return which + 1, extra

        received, rounds = lax.optimization_barrier((received, lax.pmax(rounds, "groups")))
        start = (jnp.int32(1), jnp.zeros((points, 2 * channels), BF16))
        extra = lax.while_loop(lambda state: state[0] < rounds, next_round, start)[1:]
    crossed = pl.pallas_call(
        frame_kernel if further else lambda *refs: frame_kernel(None, *refs),
        out_shape=shares,
        in_specs=[vmem] * (8 + len(extra)) + [here] * 4,
        out_specs=vmem,
        scratch_shapes=[
            *(pltpu.VMEM(array.shape[1:], BF16) for array in weights),
            pltpu.SemaphoreType.DMA((4,)),
        ],
        compiler_params=pltpu.CompilerParams(vmem_limit_bytes=(12 + points // 16) * MIB),
        name="frame_block",
    )(*extra, received, *prepared, visible, layer_gains, *weights)
    by_track = exchange(crossed)
    tracked = pl.pallas_call(
        track_kernel,
        out_shape=shares,
        in_specs=[vmem] * 7,
        out_specs=vmem,
        compiler_params=pltpu.CompilerParams(vmem_limit_bytes=(4 + points // 16) * MIB),
        name="track_block",
    )(by_track, visible, layer_gains, *weights)
    arrived = exchange(tracked)
    handed = pl.pallas_call(
        layout_kernel,
        out_shape=jax.ShapeDtypeStruct((1, points, features), BF16),
        in_specs=[vmem],
        out_specs=vmem,
        compiler_params=pltpu.CompilerParams(vmem_limit_bytes=4 * MIB),
        name="layout",
    )(arrived)
    return rounds, handed


def shards(*arrays):
    rounds, handed = step(False, *arrays)

    def again(state):
        rounds, _ = state
        return jnp.int32(1), step(True, *lax.optimization_barrier((rounds,) + arrays)[1:])[1]

    return lax.while_loop(lambda state: state[0] > 1, again, (lax.pmax(rounds, "groups"), handed))[1]


def solution(mesh):
    placed = (
        P("frame", "groups", None, None),
        P("frame", "groups"),
        P("frame", "groups"),
        P("groups"),
        P(None, "groups"),
        P("groups"),
        P(),
        P(),
        P(),
        P(),
        P(),
        P(),
    )
    return jax.shard_map(
        shards, mesh=mesh, in_specs=placed, out_specs=P("frame", "groups", None), check_vma=False
    )
```

```python
import math

import jax
import jax.numpy as jnp
from jax import lax
from jax.experimental import pallas as pl
from jax.experimental.pallas import tpu as pltpu
from jax.sharding import PartitionSpec as P

HEADS = 8
PATCH = 7
EPSILON = 1e-05
LANES = 128
TILE = 16
SPAN = 64
SHARE = 3
MIB = 1 << 20
F32 = jnp.float32
BF16 = jnp.bfloat16
VMEM = pltpu.MemorySpace.VMEM
SMEM = pltpu.MemorySpace.SMEM


def normalize(values, weights):
    average = jnp.mean(values, axis=-1, keepdims=True)
    centred = values - average
    variance = jnp.mean(centred * centred, axis=-1, keepdims=True)
    return centred * lax.rsqrt(variance + EPSILON) * weights


def iota(shape, axis):
    return lax.broadcasted_iota(jnp.int32, shape, axis)


def matmul(left, right):
    return jnp.dot(left, right, preferred_element_type=F32)


def matmul_nt(left, right):
    return lax.dot_general(left, right, (((1,), (1,)), ((), ())), preferred_element_type=F32)


def slot_cells(per_device, base, query, row, column, breadth):
    me = lax.axis_index("frame")
    points = query.shape[1]
    slots = SHARE * per_device
    mine = query == me
    before = jnp.where(iota((points, points), 0) < iota((points, points), 1), 1.0, 0.0).astype(BF16)
    rank = matmul(jnp.broadcast_to(jnp.where(mine, 1.0, 0.0), (8, points)).astype(BF16), before)[:1]
    slot = jnp.where(mine, rank.astype(jnp.int32) - base, -1)
    rows = TILE * -(-2 * slots // TILE)
    line = iota((rows, 1), 0)
    is_fine = line < slots
    held = jnp.where(is_fine, line, line - slots) == jnp.where(slot < slots, slot, -1)

    def gathered(values):
        return jnp.sum(jnp.where(held, values + 1, 0).astype(F32), axis=1, keepdims=True).astype(jnp.int32) - 1

    fine_at = gathered(row * breadth + column)
    coarse_at = gathered((row >> 1) * (breadth // 2) + (column >> 1))
    return is_fine, jnp.where(is_fine, fine_at, coarse_at)


def slot_weights(is_fine, wanted, pair, breadth):
    lane = iota((1, 2 * breadth), 1)
    column = jnp.where(lane < breadth, lane, lane - breadth)
    places = jnp.where(is_fine, lane, column >> 1)
    start = jnp.where(is_fine, pair * (2 * breadth), pair * (breadth // 2))
    return jnp.where(places == wanted - start, jnp.where(is_fine, 1.0, 0.25), 0.0).astype(BF16)


def send_block(total, out_ref):
    per_device = out_ref.shape[1]
    starts = [(level * SHARE + part) * per_device for part in range(SHARE) for level in range(2)]
    pieces = [total[start : start + per_device] for start in starts]
    block = jnp.concatenate(pieces, axis=1).astype(BF16)
    out_ref[...] = jnp.broadcast_to(block[None], out_ref.shape)


def map_copy(map_ref, cells, sems, chunk):
    depth = cells.shape[1]
    return pltpu.make_async_copy(map_ref.at[0, pl.ds(chunk * depth, depth)], cells.at[chunk], sems.at[chunk])


def each_pair(map_ref, cells, sems, body, carry):
    chunks, depth, breadth, channels = cells.shape

    def walk(chunk, carry):
        map_copy(map_ref, cells, sems, chunk).wait()
        for inner in range(depth // 2):
            both = cells[chunk, 2 * inner : 2 * inner + 2].reshape(2 * breadth, channels)
            carry = body(chunk * (depth // 2) + inner, both, carry)
        return carry

    return lax.fori_loop(0, chunks, walk, carry)


def pack_again_kernel(round_ref, query_ref, row_ref, column_ref, map_ref, out_ref, cells, sems):
    chunks, _, breadth, channels = cells.shape
    per_device = out_ref.shape[1]
    for chunk in range(chunks):
        map_copy(map_ref, cells, sems, chunk).start()
    base = round_ref[0] * SHARE * per_device
    is_fine, wanted = slot_cells(per_device, base, query_ref[...], row_ref[...], column_ref[...], breadth)

    def body(pair, both, total):
        return total + matmul(slot_weights(is_fine, wanted, pair, breadth), both)

    total = each_pair(map_ref, cells, sems, body, jnp.zeros((wanted.shape[0], channels), F32))
    send_block(total, out_ref)


def choose(query_row, devices, per_device, base):
    points = query_row.shape[1]
    across = jnp.broadcast_to(query_row.astype(F32), (points, points))
    down = across.T
    earlier = (across == down) & (iota((points, points), 1) < iota((points, points), 0))
    rank = jnp.sum(jnp.where(earlier, 1.0, 0.0), axis=1, keepdims=True).astype(jnp.int32) - base
    frame = down[:, :1].astype(jnp.int32)
    inside = (rank >= 0) & (rank < SHARE * per_device)
    at = (rank // per_device * devices + frame) * per_device + rank % per_device
    place = iota((points, SHARE * devices * per_device), 1)
    return jnp.where(place == jnp.where(inside, at, -1), 1.0, 0.0).astype(BF16)


def take(chosen, received_ref):
    devices, per_device, width = received_ref.shape
    flat = received_ref[...].reshape(devices * per_device, width)
    share = width // SHARE
    return matmul(chosen, jnp.concatenate([flat[:, g * share : (g + 1) * share] for g in range(SHARE)], axis=0))


def unpack_again_kernel(round_ref, query_ref, received_ref, before_ref, out_ref):
    devices, per_device, _ = received_ref.shape
    chosen = choose(query_ref[...], devices, per_device, round_ref[0] * SHARE * per_device)
    out_ref[...] = before_ref[...] + take(chosen, received_ref).astype(BF16)


def prepare_kernel(
    row_hbm,
    column_hbm,
    query_hbm,
    window_hbm,
    match_hbm,
    map_ref,
    packed_ref,
    rounds_ref,
    chosen_ref,
    fine_ref,
    coarse_ref,
    spread_ref,
    embedding_ref,
    row_ref,
    column_ref,
    query_ref,
    window_ref,
    match_ref,
    corners_ref,
    corner_at,
    cells,
    fine_map,
    coarse_map,
    map_sems,
    sems,
):
    chunks, depth, breadth, channels = cells.shape
    height = chunks * depth
    half = breadth // 2
    copies = [
        pltpu.make_async_copy(source, target, sems.at[index])
        for index, (source, target) in enumerate(
            (
                (row_hbm, row_ref),
                (column_hbm, column_ref),
                (query_hbm, query_ref),
                (window_hbm, window_ref),
                (match_hbm, match_ref),
            )
        )
    ]
    for copy in copies:
        copy.start()
    for chunk in range(chunks):
        map_copy(map_ref, cells, map_sems, chunk).start()
    me = lax.axis_index("frame")
    points = query_ref.shape[1]
    devices, per_device, _ = packed_ref.shape
    slots = SHARE * per_device
    place = iota((2 * SPAN, match_ref.shape[0]), 0)
    level, k, m = place >> 6, (place & (SPAN - 1)) >> 3, place & 7
    at = jnp.where((k < PATCH) & (m < PATCH), (level * PATCH + k) * PATCH + m, -1)
    pick = jnp.where(iota(place.shape, 1) == at, 1.0, 0.0).astype(BF16)
    lane = iota((half, 2 * breadth), 1)
    pool = jnp.where(jnp.where(lane < breadth, lane, lane - breadth) >> 1 == iota(lane.shape, 0), 0.25, 0.0)
    pool = pool.astype(BF16)
    coarse_map[pl.ds(height // 2 * half, 8), :] = jnp.zeros((8, channels), F32)
    features = embedding_ref.shape[1]
    feature = iota((1, features), 1)
    of_sine = feature < features // 2
    step = jnp.where(of_sine, feature, feature - features // 2).astype(F32)
    frequency = jnp.exp(-math.log(10000.0) * step / (features // 2))
    for copy in copies[:4]:
        copy.wait()
    row, column, query = row_ref[...], column_ref[...], query_ref[...]
    corners_ref[0:1, :] = row * breadth + column - (3 * breadth + 3)
    corners_ref[1:2, :] = (row >> 1) * half + (column >> 1) - (3 * half + 3)
    corner_copy = pltpu.make_async_copy(corners_ref, corner_at, sems.at[5])
    corner_copy.start()
    is_fine, wanted = slot_cells(per_device, 0, query, row, column, breadth)
    chosen_ref[...] = choose(query, devices, per_device, 0)
    there = jnp.where(iota((devices, points), 0) == query, 1.0, 0.0)
    load = jnp.max(jnp.sum(there, axis=1, keepdims=True)).astype(jnp.int32)
    rounds_ref[0] = (load + slots - 1) // slots
    copies[4].wait()
    spread_ref[...] = matmul(pick, match_ref[...]).astype(BF16)
    angle = (window_ref[0, 0] + me).astype(F32) * frequency
    embedding_ref[...] = jnp.where(of_sine, jnp.sin(angle), jnp.cos(angle))

    def convert(pair, both, total):
        product = matmul(jnp.concatenate([pool, slot_weights(is_fine, wanted, pair, breadth)], axis=0), both)
        fine_map[pl.ds(pl.multiple_of(pair * 2 * breadth, 2 * breadth), 2 * breadth), :] = both.astype(F32)
        coarse_map[pl.ds(pl.multiple_of(pair * half, half), half), :] = product[:half].astype(BF16).astype(F32)
        return total + product[half:]

    total = each_pair(map_ref, cells, map_sems, convert, jnp.zeros((wanted.shape[0], channels), F32))
    send_block(total, packed_ref)
    blank = jnp.zeros((8, channels), F32)
    corner_copy.wait()

    def gather(point, carry):
        for level, (ref, wide, out) in enumerate(((fine_map, breadth, fine_ref), (coarse_map, half, coarse_ref))):
            window = ref.at[pl.ds(corner_at[level, point], 6 * wide + 8), :]
            target = out.at[pl.ds(pl.multiple_of(point * SPAN, SPAN), SPAN), :]
            lines = [window[k * wide : k * wide + 8, :] for k in range(PATCH)] + [blank]
            for t in range(4):
                target[t * TILE : (t + 1) * TILE, :] = jnp.concatenate(lines[2 * t : 2 * t + 2], axis=0).astype(BF16)
        return carry

    lax.fori_loop(0, points, gather, 0, unroll=128)


def attention(queries, keyset, values, bias):
    rows, features = queries.shape
    per_head = features // HEADS
    head_of = iota((1, features), 1) // per_head
    spread = jnp.concatenate([jnp.where(head_of == head, queries, 0) for head in range(HEADS)], axis=0)
    scores = matmul_nt(spread, keyset)
    parts = []
    for head in range(HEADS):
        part = scores[head * rows : (head + 1) * rows] + bias
        part = part - jnp.max(part, axis=-1, keepdims=True)
        part = jnp.exp2(part * (math.log2(math.e) / math.sqrt(per_head)))
        parts.append((part * (1.0 / jnp.sum(part, axis=-1, keepdims=True))).astype(BF16))
    apart = jnp.concatenate([jnp.where(head_of == head, values, 0) for head in range(HEADS)], axis=0)
    return matmul(jnp.concatenate(parts, axis=1), apart).astype(BF16)


def gelu(value):
    inner = math.sqrt(2.0 / math.pi)
    lifted = value * (inner + (inner * 0.044715) * (value * value))
    half = 0.5 * value
    return half + half * jnp.tanh(lifted)


def finish(stream, attended, gain, output_weight, expand_weight, reduce_weight):
    stream = stream + matmul(attended, output_weight())
    hidden = normalize(stream, gain).astype(BF16)
    widened = gelu(matmul(hidden, expand_weight())).astype(BF16)
    return stream + matmul(widened, reduce_weight())


def frame_kernel(
    extra_ref,
    received_ref,
    chosen_ref,
    fine_ref,
    coarse_ref,
    spread_ref,
    embedding_ref,
    visible_ref,
    gains_ref,
    *refs,
):
    sources, out_ref, held, sems = refs[:4], refs[4], refs[5:9], refs[9]
    copies = [
        pltpu.make_async_copy(source.at[0], target, sems.at[index])
        for index, (source, target) in enumerate(zip(sources, held))
    ]
    for copy in copies:
        copy.start()

    def weight(index):
        def ready():
            copies[index].wait()
            return held[index][...]

        return ready

    me = lax.axis_index("frame")
    points = visible_ref.shape[1]
    channels = fine_ref.shape[1]
    features = spread_ref.shape[1]
    anchors = take(chosen_ref[...], received_ref)
    if extra_ref is not None:
        anchors = anchors + extra_ref[...].astype(F32)
    line, lane = iota((8, LANES), 0), iota((8, LANES), 1)
    none = jnp.zeros((8, channels), F32)
    rows = []
    for start in range(0, points, 8):
        fine, coarse = anchors[start : start + 8, :channels], anchors[start : start + 8, channels:]
        both = jnp.concatenate(
            [jnp.concatenate([fine, none], axis=1), jnp.concatenate([none, coarse], axis=1)], axis=0
        ).astype(BF16)
        span = slice(start * SPAN, (start + 8) * SPAN)
        scores = matmul_nt(both, jnp.concatenate([fine_ref[span, :], coarse_ref[span, :]], axis=1))
        sides = []
        for level in range(2):
            own = scores[level * 8 : level * 8 + 8]
            kept = own[:, :LANES]
            for index in range(1, 4):
                kept = jnp.where(line // 2 == index, own[:, index * LANES : (index + 1) * LANES], kept)
            sides.append(jnp.where(line % 2 == level, kept, pltpu.roll(kept, SPAN, 1)))
        rows.append(jnp.where(lane < SPAN, sides[0], sides[1]))
    matches = (jnp.concatenate(rows, axis=0) * (1.0 / math.sqrt(channels))).astype(BF16)
    tokens = (matmul(matches, spread_ref[...]) + embedding_ref[...]).astype(BF16)

    stream = tokens.astype(F32)
    hidden = normalize(stream, gains_ref[0, 0:1, :]).astype(BF16)
    projected = matmul(hidden, weight(0)()).astype(BF16)
    allowed = visible_ref[pl.ds(me, 1), :] == 1
    permitted = allowed | (iota((points, points), 0) == iota((points, points), 1))
    attended = attention(
        projected[:, :features],
        projected[:, features : 2 * features],
        projected[:, 2 * features :],
        jnp.where(permitted, 0.0, -1e30),
    )
    crossed = finish(stream, attended, gains_ref[0, 1:2, :], weight(1), weight(2), weight(3))
    out_ref[...] = crossed.astype(BF16).reshape(out_ref.shape)


def track_kernel(received_ref, visible_ref, gains_ref, joint_ref, output_ref, expand_ref, reduce_ref, out_ref):
    me = lax.axis_index("frame")
    length, per_device, features = received_ref.shape
    points = visible_ref.shape[1]
    half_way = length // 2
    rest = length - half_way
    total = length * per_device
    skipped = half_way * per_device
    stream = received_ref[...].astype(F32).reshape(total, features)
    hidden = normalize(stream, gains_ref[1, 0:1, :]).astype(BF16)
    projected = matmul(hidden, joint_ref[1]).astype(BF16)
    pick = iota((points, total), 0) == me * per_device + iota((points, total), 1) % per_device
    seen = matmul(jnp.where(visible_ref[...] == 1, 1.0, 0.0).astype(BF16), jnp.where(pick, 1.0, 0.0).astype(BF16))
    seen = jnp.where(iota((length, total), 1) // per_device == iota((length, total), 0), seen, 0.0)
    allowed = jnp.sum(seen, axis=0, keepdims=True) > 0.5
    query_at = iota((rest * per_device, total), 0) + skipped
    key_at = iota((rest * per_device, total), 1)
    same_point = query_at % per_device == key_at % per_device
    permitted = same_point & (allowed | (query_at == key_at))
    attended = attention(
        projected[skipped:, :features],
        projected[:, features : 2 * features],
        projected[:, 2 * features :],
        jnp.where(permitted, 0.0, -1e30),
    )
    tracked = finish(
        stream[skipped:],
        attended,
        gains_ref[1, 1:2, :],
        lambda: output_ref[1],
        lambda: expand_ref[1],
        lambda: reduce_ref[1],
    )
    tracked = tracked.astype(BF16).reshape(rest, per_device, features)
    out_ref[:rest] = tracked
    out_ref[rest:] = jnp.broadcast_to(tracked[rest - 1 :], (half_way, per_device, features))


def layout_kernel(received_ref, out_ref):
    out_ref[...] = received_ref[...].astype(F32).reshape(out_ref.shape).astype(BF16)


def exchange(block):
    return lax.all_to_all(block, "frame", split_axis=0, concat_axis=0, tiled=True)


def step(
    further,
    feature_map,
    pixel_row,
    pixel_column,
    query_frame,
    visible,
    window_start,
    match_weight,
    layer_gains,
    *weights,
):
    _, height, breadth, channels = feature_map.shape
    points = query_frame.shape[0]
    features = match_weight.shape[1]
    devices = lax.axis_size("frame")
    per_device = points // devices
    query_row = query_frame.reshape(1, points)
    vmem = pl.BlockSpec(memory_space=VMEM)
    smem = pl.BlockSpec(memory_space=SMEM)
    here = pl.BlockSpec(memory_space=pltpu.MemorySpace.HBM)
    chunks = 8
    map_scratch = pltpu.VMEM((chunks, height // chunks, breadth, channels), BF16)
    map_sems = pltpu.SemaphoreType.DMA((chunks,))
    block = jax.ShapeDtypeStruct((devices, per_device, SHARE * 2 * channels), BF16)
    shares = jax.ShapeDtypeStruct((devices, per_device, features), BF16)

    line = pltpu.VMEM((1, points), jnp.int32)
    packed, rounds, *prepared = pl.pallas_call(
        prepare_kernel,
        out_shape=[
            block,
            jax.ShapeDtypeStruct((1,), jnp.int32),
            jax.ShapeDtypeStruct((points, SHARE * devices * per_device), BF16),
            jax.ShapeDtypeStruct((points * SPAN, channels), BF16),
            jax.ShapeDtypeStruct((points * SPAN, channels), BF16),
            jax.ShapeDtypeStruct((2 * SPAN, features), BF16),
            jax.ShapeDtypeStruct((1, features), F32),
        ],
        in_specs=[here] * 6,
        out_specs=[vmem, smem] + [vmem] * 5,
        scratch_shapes=[
            line,
            line,
            line,
            pltpu.SMEM((1, 1), jnp.int32),
            pltpu.VMEM(match_weight.shape, BF16),
            pltpu.VMEM((2, points), jnp.int32),
            pltpu.SMEM((2, points), jnp.int32),
            map_scratch,
            pltpu.VMEM((height * breadth, channels), F32),
            pltpu.VMEM((height * breadth // 4 + 8, channels), F32),
            map_sems,
            pltpu.SemaphoreType.DMA((6,)),
        ],
        compiler_params=pltpu.CompilerParams(vmem_limit_bytes=(16 + points // 16) * MIB),
        name="prepare",
    )(pixel_row, pixel_column, query_row, window_start.reshape(1, 1), match_weight, feature_map)
    rounds = rounds.reshape(())
    received = exchange(packed)
    extra = ()
    if further:

        def next_round(state):
            which, extra = state
            again = pl.pallas_call(
                pack_again_kernel,
                out_shape=block,
                in_specs=[smem, vmem, vmem, vmem, here],
                out_specs=vmem,
                scratch_shapes=[map_scratch, map_sems],
                compiler_params=pltpu.CompilerParams(vmem_limit_bytes=8 * MIB),
                name="pack_again",
            )(which.reshape(1), query_row, pixel_row, pixel_column, feature_map)
            extra = pl.pallas_call(
                unpack_again_kernel,
                out_shape=jax.ShapeDtypeStruct(extra.shape, BF16),
                in_specs=[smem, vmem, vmem, vmem],
                out_specs=vmem,
                compiler_params=pltpu.CompilerParams(vmem_limit_bytes=(4 + points // 16) * MIB),
                name="unpack_again",
            )(which.reshape(1), query_row, exchange(again), extra)
            return which + 1, extra

        received, rounds = lax.optimization_barrier((received, lax.pmax(rounds, "groups")))
        start = (jnp.int32(1), jnp.zeros((points, 2 * channels), BF16))
        extra = lax.while_loop(lambda state: state[0] < rounds, next_round, start)[1:]
    crossed = pl.pallas_call(
        frame_kernel if further else lambda *refs: frame_kernel(None, *refs),
        out_shape=shares,
        in_specs=[vmem] * (8 + len(extra)) + [here] * 4,
        out_specs=vmem,
        scratch_shapes=[
            *(pltpu.VMEM(array.shape[1:], BF16) for array in weights),
            pltpu.SemaphoreType.DMA((4,)),
        ],
        compiler_params=pltpu.CompilerParams(vmem_limit_bytes=(12 + points // 16) * MIB),
        name="frame_block",
    )(*extra, received, *prepared, visible, layer_gains, *weights)
    by_track = exchange(crossed)
    tracked = pl.pallas_call(
        track_kernel,
        out_shape=shares,
        in_specs=[vmem] * 7,
        out_specs=vmem,
        compiler_params=pltpu.CompilerParams(vmem_limit_bytes=(4 + points // 16) * MIB),
        name="track_block",
    )(by_track, visible, layer_gains, *weights)
    arrived = exchange(tracked)
    handed = pl.pallas_call(
        layout_kernel,
        out_shape=jax.ShapeDtypeStruct((1, points, features), BF16),
        in_specs=[vmem],
        out_specs=vmem,
        compiler_params=pltpu.CompilerParams(vmem_limit_bytes=4 * MIB),
        name="layout",
    )(arrived)
    return rounds, handed


def shards(*arrays):
    rounds, handed = step(False, *arrays)

    def again(state):
        rounds, _ = state
        return jnp.int32(1), step(True, *lax.optimization_barrier((rounds,) + arrays)[1:])[1]

    return lax.while_loop(lambda state: state[0] > 1, again, (lax.pmax(rounds, "groups"), handed))[1]


def solution(mesh):
    placed = (
        P("frame", "groups", None, None),
        P("frame", "groups"),
        P("frame", "groups"),
        P("groups"),
        P(None, "groups"),
        P("groups"),
        P(),
        P(),
        P(),
        P(),
        P(),
        P(),
    )
    return jax.shard_map(
        shards, mesh=mesh, in_specs=placed, out_specs=P("frame", "groups", None), check_vma=False
    )
```
